256 devices in a mesh: seq: 16 (over x, y), head: 16 (over z, core).
Axes of the slice: x: 4, y: 4, z: 8, core: 2. Of those that a mesh axis runs over, the one named last changes fastest.
Arguments:
- queries: bfloat16 [16384, 4096], P('seq', 'head'), may hold values from -100 to 100
- states: bfloat16 [4096, 8192], P('seq', 'head'), may hold values from -6 to 6
- key_weight: bfloat16 [8192, 4096], P(None, 'head'), may hold values from -0.0625 to 0.0625
- value_weight: bfloat16 [8192, 4096], P(None, 'head'), may hold values from -0.0625 to 0.0625
- neighbour_ids: int32 [256, 2], P('seq'), may hold values from 0 to 31, all different within a row
- out_grad: bfloat16 [16384, 4096], P('seq', 'head'), may hold values from -4 to 4
Outputs:
- context: bfloat16 [16384, 4096], P('seq', 'head')
- query_grad: bfloat16 [16384, 4096], P('seq', 'head')
- key_weight_grad: float32 [8192, 4096], P('seq', 'head')
- value_weight_grad: float32 [8192, 4096], P('seq', 'head')
The draws below stay inside these ranges and needn't reach their ends.
Inputs may be any that keep to these rules, and one draw needn't show every extreme that they name: `neighbour_ids`: each span names 2 different pool blocks, and every block is named by some span.
All inputs are finite; a program needn't handle non-finite values.
Results may differ from the reference program's by a relative error of at most 0.04.
Values may be sent and summed in bfloat16 or wider, within the bound.
A program may use at most 128 MiB of HBM per device.

```python
import math
import jax
import jax.numpy as jnp
from jax import lax

D = 8192
HD = 128
HEADS = 32
SPAN = 64
NBR = 128
TOPN = 2
TOK_DEV = 1024
BLK_DEV = 2
TOKENS = 16384
SPANS = 256
BLOCKS = 32
POOL = 4096
HH = 4096
N_SEQ = 16


def draw_queries(key, part):
    first_key = jax.random.fold_in(key, 11)
    drawn = jax.random.normal(first_key, (TOKENS, HEADS * HD), jnp.float32)
    return jnp.clip(drawn, -100.0, 100.0).astype(jnp.bfloat16)


def shard_levels(stream_key, shape, shards, smallest, high):
    loudness, own = 1.0, jax.random.fold_in(stream_key, 6)
    for position, blocks in shards:
        steps = jnp.exp(jax.random.uniform(jax.random.fold_in(own, position), (blocks,), jnp.float32, smallest / len(shards), high / len(shards)))
        loudness = loudness * jnp.repeat(steps, shape[position] // blocks).reshape([-1 if axis == position else 1 for axis in range(len(shape))])
    return loudness


def picks_of(own_key, rows, amount, top, lift):
    ranking = jax.random.permutation(jax.random.fold_in(own_key, 1), amount)
    favour = ranking
    for power in range(3):
        favour = favour * favour // amount
    favour = favour * lift // amount
    lots = jax.random.randint(jax.random.fold_in(own_key, 2), (rows, amount), 0, 4096) + favour
    fixed_rows = jax.random.permutation(jax.random.fold_in(own_key, 3), rows)[jnp.arange(amount) % rows]
    lots = jnp.where(jnp.arange(rows)[:, None] == fixed_rows[None, :], 1 << 14, lots)
    priority = lots * amount + jnp.arange(amount)
    return lax.top_k(priority.astype(jnp.int32), top)[1].astype(jnp.int32)


def scatter_about(rng, shape, spread, most, shards=(), held_as=jnp.bfloat16):
    values = jax.random.normal(rng, shape, jnp.float32) * spread
    if len(shards) > 0:
        values = shard_levels(rng, shape, shards, -0.22, 0.18) * values
    return jnp.clip(values, min=-most, max=most).astype(held_as)


def setup_inputs(seed: int = 0) -> dict:
    splits = jax.random.split(jax.random.key(seed), 7)
    return {
        "queries": draw_queries(jax.random.fold_in(splits[6], 71), 0),
        "states": scatter_about(splits[1], (POOL, D), 1.0, 6.0, ((0, 16), (1, 16))),
        "key_weight": scatter_about(splits[2], (D, HH), D ** -0.5, 0.0625, ((1, 16),)),
        "value_weight": scatter_about(splits[3], (D, HH), D ** -0.5, 0.0625, ((1, 16),)),
        "neighbour_ids": picks_of(splits[4], SPANS, BLOCKS, TOPN, 1024),
        "out_grad": scatter_about(splits[5], (TOKENS, HH), 0.5, 4.0, ((0, 16), (1, 16))),
    }


def attend(queries_here, grad_here, key_rows, value_rows):
    score_scale = 1.0 / math.sqrt(HD)
    query_f = queries_here.astype(jnp.float32)
    key_f = key_rows.astype(jnp.float32)
    value_f = value_rows.astype(jnp.float32)
    grad_f = grad_here.astype(jnp.float32)
    scores = jnp.einsum('qhd,khd->hqk', query_f, key_f) * score_scale
    soft_weights = jax.nn.softmax(scores, axis=-1)
    weights_low = lax.optimization_barrier(soft_weights.astype(jnp.bfloat16)).astype(jnp.float32)
    context = jnp.einsum('hqk,khd->qhd', weights_low, value_f).astype(jnp.bfloat16)
    prob_grad = jnp.einsum('qhd,khd->hqk', grad_f, value_f)
    row_delta = lax.optimization_barrier(jnp.sum(soft_weights * prob_grad, axis=-1, keepdims=True))
    score_grad = (soft_weights * (prob_grad - row_delta) * score_scale).astype(jnp.bfloat16)
    score_grad = lax.optimization_barrier(score_grad).astype(jnp.float32)
    query_grad = jnp.einsum('hqk,khd->qhd', score_grad, key_f).astype(jnp.bfloat16)
    key_part = jnp.einsum('hqk,qhd->khd', score_grad, query_f)
    value_part = jnp.einsum('hqk,qhd->khd', weights_low, grad_f)
    return (context, query_grad, key_part, value_part)

def reference(queries, states, key_weight, value_weight, neighbour_ids, out_grad):
    pool_keys = jnp.dot(states, key_weight, preferred_element_type=jnp.float32).astype(jnp.bfloat16)
    pool_values = jnp.dot(states, value_weight, preferred_element_type=jnp.float32).astype(jnp.bfloat16)
    key_blocks = pool_keys.reshape(BLOCKS, NBR, HEADS, HD)
    value_blocks = pool_values.reshape(BLOCKS, NBR, HEADS, HD)
    per_group = TOK_DEV // SPAN
    query_groups = queries.reshape(N_SEQ, per_group, SPAN, HEADS, HD)
    grad_groups = out_grad.reshape(N_SEQ, per_group, SPAN, HEADS, HD)
    id_groups = neighbour_ids.reshape(N_SEQ, per_group, TOPN)
    block_range = jnp.arange(BLOCKS, dtype=jnp.int32)

    def one_span(inputs):
        queries_here, grad_here, span_ids = inputs
        key_rows = key_blocks[span_ids].reshape(TOPN * NBR, HEADS, HD)
        value_rows = value_blocks[span_ids].reshape(TOPN * NBR, HEADS, HD)
        return attend(queries_here, grad_here, key_rows, value_rows)

    def one_group(totals, inputs):
        queries_here, grad_here, span_ids = inputs
        context, query_grad, key_part, value_part = lax.map(one_span, (queries_here, grad_here, span_ids))
        block_picks = (span_ids.reshape(-1)[:, None] == block_range[None, :]).astype(jnp.float32)
        key_flat = key_part.reshape(per_group * TOPN, NBR * HEADS * HD)
        value_flat = value_part.reshape(per_group * TOPN, NBR * HEADS * HD)
        key_sum = jnp.dot(block_picks.T, key_flat, precision=lax.Precision.HIGHEST)
        value_sum = jnp.dot(block_picks.T, value_flat, precision=lax.Precision.HIGHEST)
        key_sum = lax.optimization_barrier(key_sum.astype(jnp.bfloat16)).astype(jnp.float32)
        value_sum = lax.optimization_barrier(value_sum.astype(jnp.bfloat16)).astype(jnp.float32)
        return ((totals[0] + key_sum, totals[1] + value_sum), (context, query_grad))
    zero_sums = jnp.zeros((BLOCKS, NBR * HEADS * HD), jnp.float32)
    (key_total, value_total), (context, query_grad) = lax.scan(one_group, (zero_sums, zero_sums), (query_groups, grad_groups, id_groups))
    key_pool = key_total.astype(jnp.bfloat16).reshape(N_SEQ, BLK_DEV * NBR, HEADS * HD)
    value_pool = value_total.astype(jnp.bfloat16).reshape(N_SEQ, BLK_DEV * NBR, HEADS * HD)
    state_groups = states.reshape(N_SEQ, BLK_DEV * NBR, D)

    def weight_group(totals, inputs):
        state_rows, key_rows, value_rows = inputs
        key_term = jnp.dot(state_rows.T, key_rows, preferred_element_type=jnp.float32)
        value_term = jnp.dot(state_rows.T, value_rows, preferred_element_type=jnp.float32)
        key_term = lax.optimization_barrier(key_term.astype(jnp.bfloat16)).astype(jnp.float32)
        value_term = lax.optimization_barrier(value_term.astype(jnp.bfloat16)).astype(jnp.float32)
        return ((totals[0] + key_term, totals[1] + value_term), None)
    zero_grad = jnp.zeros((D, HEADS * HD), jnp.float32)
    (key_weight_grad, value_weight_grad), unused = lax.scan(weight_group, (zero_grad, zero_grad), (state_groups, key_pool, value_pool))
    return (context.reshape(TOKENS, HEADS * HD), query_grad.reshape(TOKENS, HEADS * HD), key_weight_grad, value_weight_grad)
```

```python
import math

import jax
import jax.numpy as jnp
from jax import lax
from jax.experimental import pallas as pl
from jax.experimental.pallas import tpu as pltpu
from jax.sharding import PartitionSpec as P

HD = 128
SPAN = 64
NBR = 128
TOPN = 2
SCALE = 1.0 / math.sqrt(HD)
MIB = 1 << 20


def dot_nt(a, b):
    return lax.dot_general(a, b, (((1,), (1,)), ((), ())), preferred_element_type=jnp.float32)


def dot_tn(a, b):
    return lax.dot_general(a, b, (((0,), (0,)), ((), ())), preferred_element_type=jnp.float32)


def dot_nn(a, b):
    return jnp.dot(a, b, preferred_element_type=jnp.float32)


def attend_kernel(ids_ref, q_ref, g_ref, kv_ref, ctx_ref, dq_ref, dkv_ref, acc_ref):
    cols = q_ref.shape[1]
    spans = q_ref.shape[0] // SPAN
    pool = kv_ref.shape[0]
    first = lax.broadcasted_iota(jnp.int32, (SPAN, cols), 1) < HD

    def clear(i, _):
        acc_ref[pl.ds(i * NBR, NBR), :] = jnp.zeros((NBR, 2 * cols), jnp.float32)
        return 0

    lax.fori_loop(0, pool // NBR, clear, 0)

    def stack(x):
        zero = jnp.zeros_like(x)
        return jnp.concatenate([jnp.where(first, x, zero), jnp.where(first, zero, x)], axis=0)

    def unstack(x):
        return jnp.where(first, x[:SPAN], x[SPAN:])

    def span(c, _):
        rows = pl.ds(c * SPAN, SPAN)
        at0 = pl.ds(ids_ref[c, 0] * NBR, NBR)
        at1 = pl.ds(ids_ref[c, 1] * NBR, NBR)
        keys = jnp.concatenate([kv_ref[at0, :cols], kv_ref[at1, :cols]], axis=0)
        values = jnp.concatenate([kv_ref[at0, cols:], kv_ref[at1, cols:]], axis=0)
        q2 = stack(q_ref[rows, :])
        g2 = stack(g_ref[rows, :])
        scores = dot_nt(q2, keys) * SCALE
        prob_grad = dot_nt(g2, values)
        top = jnp.max(scores, axis=-1, keepdims=True)
        e = jnp.exp(scores - top)
        probs = e / jnp.sum(e, axis=-1, keepdims=True)
        low = probs.astype(jnp.bfloat16)
        delta = jnp.sum(probs * prob_grad, axis=-1, keepdims=True)
        sg = (probs * (prob_grad - delta) * SCALE).astype(jnp.bfloat16)
        ctx_ref[rows, :] = unstack(dot_nn(low, values)).astype(jnp.bfloat16)
        dq_ref[rows, :] = unstack(dot_nn(sg, keys)).astype(jnp.bfloat16)
        dk = dot_tn(sg, q2)
        dv = dot_tn(low, g2)
        acc_ref[at0, :cols] += dk[:NBR]
        acc_ref[at0, cols:] += dv[:NBR]
        acc_ref[at1, :cols] += dk[NBR:]
        acc_ref[at1, cols:] += dv[NBR:]
        return 0

    lax.fori_loop(0, spans, span, 0)

    def store(i, _):
        at = pl.ds(i * NBR, NBR)
        dkv_ref[at, :] = acc_ref[at, :].astype(jnp.bfloat16)
        return 0

    lax.fori_loop(0, pool // NBR, store, 0)


def attend(ids, queries, grads, kv):
    rows, cols = queries.shape
    pool = kv.shape[0]
    vmem = pl.BlockSpec(memory_space=pltpu.VMEM)
    return pl.pallas_call(
        attend_kernel,
        out_shape=(
            jax.ShapeDtypeStruct((rows, cols), jnp.bfloat16),
            jax.ShapeDtypeStruct((rows, cols), jnp.bfloat16),
            jax.ShapeDtypeStruct((pool, 2 * cols), jnp.bfloat16),
        ),
        in_specs=[pl.BlockSpec(memory_space=pltpu.SMEM), vmem, vmem, vmem],
        out_specs=(vmem, vmem, vmem),
        scratch_shapes=[pltpu.VMEM((pool, 2 * cols), jnp.float32)],
        compiler_params=pltpu.CompilerParams(vmem_limit_bytes=40 * MIB),
        name="attend",
    )(ids, queries, grads, kv)


def local(queries, states, key_weight, value_weight, neighbour_ids, out_grad):
    cols = queries.shape[1]
    full_states = lax.all_gather(states, "head", axis=1, tiled=True)
    keys = dot_nn(full_states, key_weight).astype(jnp.bfloat16)
    values = dot_nn(full_states, value_weight).astype(jnp.bfloat16)
    own = jnp.concatenate([keys, values], axis=1)
    kv = lax.all_gather(own, "seq", axis=0, tiled=True)
    context, query_grad, dkv = attend(neighbour_ids, queries, out_grad, kv)
    own_grad = lax.psum_scatter(dkv, "seq", scatter_dimension=0, tiled=True)
    grads = lax.psum_scatter(
        dot_tn(full_states, own_grad).astype(jnp.bfloat16), "seq", scatter_dimension=0, tiled=True
    ).astype(jnp.float32)
    return context, query_grad, grads[:, :cols], grads[:, cols:]


def solution(mesh):
    in_specs = (
        P("seq", "head"),
        P("seq", "head"),
        P(None, "head"),
        P(None, "head"),
        P("seq", None),
        P("seq", "head"),
    )
    out_specs = (P("seq", "head"), P("seq", "head"), P("seq", "head"), P("seq", "head"))
    return jax.shard_map(local, mesh=mesh, in_specs=in_specs, out_specs=out_specs, check_vma=False)
```

```python
import math

import jax
import jax.numpy as jnp
from jax import lax
from jax.experimental import pallas as pl
from jax.experimental.pallas import tpu as pltpu
from jax.sharding import PartitionSpec as P

HD = 128
SPAN = 64
NBR = 128
TOPN = 2
SCALE = 1.0 / math.sqrt(HD)
MIB = 1 << 20
MESH = pl.DeviceIdType.MESH
SIDE = 4
RING = 8


def dot_nt(a, b):
    return lax.dot_general(a, b, (((1,), (1,)), ((), ())), preferred_element_type=jnp.float32)


def dot_tn(a, b):
    return lax.dot_general(a, b, (((0,), (0,)), ((), ())), preferred_element_type=jnp.float32)


def dot_nn(a, b):
    return jnp.dot(a, b, preferred_element_type=jnp.float32)


def attend_kernel(ids_ref, q_ref, g_ref, kv_ref, ctx_ref, dq_ref, dkv_ref, acc_ref):
    cols = q_ref.shape[1]
    spans = q_ref.shape[0] // SPAN
    blocks = kv_ref.shape[1]
    first = lax.broadcasted_iota(jnp.int32, (SPAN, cols), 1) < HD

    def clear(i, _):
        for j in range(2):
            acc_ref[j, i] = jnp.zeros((NBR, cols), jnp.float32)
        return 0

    lax.fori_loop(0, blocks, clear, 0)

    def stack(x):
        zero = jnp.zeros_like(x)
        return jnp.concatenate([jnp.where(first, x, zero), jnp.where(first, zero, x)], axis=0)

    def unstack(x):
        return jnp.where(first, x[:SPAN], x[SPAN:])

    def span(c, _):
        rows = pl.ds(c * SPAN, SPAN)
        id0, id1 = ids_ref[c, 0], ids_ref[c, 1]
        keys = jnp.concatenate([kv_ref[0, id0], kv_ref[0, id1]], axis=0)
        values = jnp.concatenate([kv_ref[1, id0], kv_ref[1, id1]], axis=0)
        q2 = stack(q_ref[rows, :])
        g2 = stack(g_ref[rows, :])
        scores = dot_nt(q2, keys) * SCALE
        prob_grad = dot_nt(g2, values)
        top = jnp.max(scores, axis=-1, keepdims=True)
        e = jnp.exp(scores - top)
        probs = e / jnp.sum(e, axis=-1, keepdims=True)
        low = probs.astype(jnp.bfloat16)
        delta = jnp.sum(probs * prob_grad, axis=-1, keepdims=True)
        sg = (probs * (prob_grad - delta) * SCALE).astype(jnp.bfloat16)
        ctx_ref[rows, :] = unstack(dot_nn(low, values)).astype(jnp.bfloat16)
        dq_ref[rows, :] = unstack(dot_nn(sg, keys)).astype(jnp.bfloat16)
        dk = dot_tn(sg, q2)
        dv = dot_tn(low, g2)
        acc_ref[0, id0] += dk[:NBR]
        acc_ref[1, id0] += dv[:NBR]
        acc_ref[0, id1] += dk[NBR:]
        acc_ref[1, id1] += dv[NBR:]
        return 0

    lax.fori_loop(0, spans, span, 0)

    def store(i, _):
        for j in range(2):
            dkv_ref[j, i] = acc_ref[j, i].astype(jnp.bfloat16)
        return 0

    lax.fori_loop(0, blocks, store, 0)


def attend(ids, queries, grads, kv):
    rows, cols = queries.shape
    blocks = kv.shape[1] * kv.shape[2] // NBR
    vmem = pl.BlockSpec(memory_space=pltpu.VMEM)
    context, query_grad, dkv = pl.pallas_call(
        attend_kernel,
        out_shape=(
            jax.ShapeDtypeStruct((rows, cols), jnp.bfloat16),
            jax.ShapeDtypeStruct((rows, cols), jnp.bfloat16),
            jax.ShapeDtypeStruct((2, blocks, NBR, cols), jnp.bfloat16),
        ),
        in_specs=[pl.BlockSpec(memory_space=pltpu.SMEM), vmem, vmem, vmem],
        out_specs=(vmem, vmem, vmem),
        scratch_shapes=[pltpu.VMEM((2, blocks, NBR, cols), jnp.float32)],
        compiler_params=pltpu.CompilerParams(vmem_limit_bytes=40 * MIB),
        name="attend",
    )(ids, queries, grads, kv.reshape(2, blocks, NBR, cols))
    return context, query_grad, dkv.reshape(kv.shape)


def wrap(i, n):
    return lax.rem(i + n, n)


class Place:
    def __init__(self):
        self.seq = lax.axis_index("seq")
        self.head = lax.axis_index("head")
        self.x, self.y = self.seq // SIDE, lax.rem(self.seq, SIDE)
        self.z, self.core = self.head // 2, lax.rem(self.head, 2)

    def along(self, is_x, step):
        if is_x:
            return (wrap(self.x + step, SIDE) * SIDE + self.y, self.head)
        return (self.x * SIDE + wrap(self.y + step, SIDE), self.head)

    def ring(self, step):
        return (self.seq, wrap(self.z + step, RING) * 2 + self.core)

    def twin(self):
        return (self.seq, self.z * 2 + 1 - self.core)

    def slot(self, first_is_x, first, second):
        if first_is_x:
            return wrap(self.x + first, SIDE) * SIDE + wrap(self.y + second, SIDE)
        return wrap(self.x + second, SIDE) * SIDE + wrap(self.y + first, SIDE)


def greet(devices):
    barrier = pltpu.get_barrier_semaphore()
    for device in devices:
        pl.semaphore_signal(barrier, inc=1, device_id=device, device_id_type=MESH)
    pl.semaphore_wait(barrier, len(devices))


class Sender:
    def __init__(self, sems):
        self.sems, self.started = sems, []

    def send(self, src, dst, recv_sem, device):
        copy = pltpu.make_async_remote_copy(
            src_ref=src,
            dst_ref=dst,
            send_sem=self.sems.at[len(self.started)],
            recv_sem=recv_sem,
            device_id=device,
            device_id_type=MESH,
        )
        copy.start()
        self.started.append(copy)

    def finish(self):
        for copy in self.started:
            copy.wait_send()


def arrived(ref, send_sem, recv_sem, device):
    pltpu.make_async_remote_copy(
        src_ref=ref, dst_ref=ref, send_sem=send_sem, recv_sem=recv_sem, device_id=device, device_id_type=MESH
    ).wait_recv()


class Gather:
    def __init__(self, place, sender, buf, recv, j, first_is_x, cid, row, rows, sign):
        self.place, self.sender, self.buf, self.recv = place, sender, buf, recv
        self.j, self.fx, self.cid, self.row, self.rows, self.sign = j, first_is_x, cid, row, rows, sign

    def ref(self, slot):
        return self.buf.at[self.j, slot, pl.ds(self.row, self.rows), :]

    def send(self, offsets, is_x, step):
        slot = self.place.slot(self.fx, *offsets)
        self.sender.send(
            self.ref(slot), self.ref(slot), self.recv.at[self.j, slot, self.cid], self.place.along(is_x, step)
        )

    def wait(self, offsets):
        slot = self.place.slot(self.fx, *offsets)
        arrived(self.ref(slot), self.sender.sems.at[0], self.recv.at[self.j, slot, self.cid], self.place.twin())

    def spread(self, first):
        self.send((first, 0), not self.fx, self.sign)
        self.send((first, 0), not self.fx, -self.sign)

    def begin(self):
        self.send((0, 0), self.fx, self.sign)
        self.send((0, 0), self.fx, -self.sign)
        self.spread(0)

    def near(self):
        self.wait((-self.sign, 0))
        self.send((-self.sign, 0), self.fx, self.sign)
        self.spread(-self.sign)
        self.wait((self.sign, 0))
        self.spread(self.sign)

    def far(self):
        self.wait((-2 * self.sign, 0))
        self.spread(2)

    def relay(self, first):
        self.wait((first, -self.sign))
        self.send((first, -self.sign), not self.fx, self.sign)

    def relays(self):
        return [0, -self.sign, self.sign, 2]

    def end(self):
        for first in self.relays():
            self.wait((first, self.sign))
            self.wait((first, 2))


def pool_kernel(states_ref, kw_ref, vw_ref, kv_ref, part_ref, st, w, acc, send_sems, twin_recv, ring_recv, pool_recv, w_sems):
    place = Place()
    heads, rows, feats = st.shape
    cols = kv_ref.shape[3]
    half = rows // 2
    loads = [pltpu.make_async_copy(kw_ref, w.at[0], w_sems.at[0]), pltpu.make_async_copy(vw_ref, w.at[1], w_sems.at[1])]
    for load in loads:
        load.start()
    st[place.head] = states_ref[...]
    acc[...] = jnp.zeros_like(acc)
    greet([place.ring(1), place.ring(-1), place.twin()] + [place.along(i, d) for i in (True, False) for d in (1, -1)])
    sender = Sender(send_sems)

    def ref(slot, g):
        return st.at[slot, pl.ds(g * half, half), :]

    def slot_at(distance, other):
        core = 1 - place.core if other else place.core
        return wrap(place.z + distance, RING) * 2 + core

    def to_ring(slot, g, sign):
        sender.send(ref(slot, g), ref(slot, g), ring_recv.at[slot, g], place.ring(sign))

    def to_twin(slot, g):
        sender.send(ref(slot, g), ref(slot, g), twin_recv.at[slot, g], place.twin())

    def multiply(slot, g):
        at = pl.ds(g * half, half)
        left = st[slot, at, :]
        acc[at, :cols] += dot_nn(left, w[0, slot])
        acc[at, cols:] += dot_nn(left, w[1, slot])

    def signs(d, g):
        return (1, -1) if d < RING // 2 else ((1,) if g == 0 else (-1,))

    def hop(g, d):
        for sign in signs(d, g):
            slot = slot_at(-sign * d, False)
            arrived(ref(slot, g), send_sems.at[0], ring_recv.at[slot, g], place.twin())
            if sign in signs(d + 1, g) and d < RING // 2:
                to_ring(slot, g, sign)
            to_twin(slot, g)

    def own(g, d):
        for sign in signs(d, g) if d else (1,):
            multiply(slot_at(-sign * d, False), g)

    def other(g, d):
        for sign in signs(d, g) if d else (1,):
            slot = slot_at(-sign * d, True)
            arrived(ref(slot, g), send_sems.at[0], twin_recv.at[slot, g], place.twin())
            multiply(slot, g)

    def project(g):
        at = pl.ds(g * half, half)
        kv_ref[0, place.seq, at, :] = acc[at, :cols].astype(kv_ref.dtype)
        kv_ref[1, place.seq, at, :] = acc[at, cols:].astype(kv_ref.dtype)

    def gathers(g):
        quarter = half // 2
        return [
            Gather(place, sender, kv_ref, pool_recv, j, j == 0, 2 * g + i, g * half + i * quarter, quarter, sign)
            for i, sign in enumerate((1, -1))
            for j in range(2)
        ]

    for g in range(2):
        for sign in (1, -1):
            to_ring(place.head, g, sign)
        to_twin(place.head, g)
    for load in loads:
        load.wait()
    hop(0, 1)
    own(0, 0)
    hop(1, 1)
    hop(0, 2)
    other(0, 0)
    own(0, 1)
    hop(1, 2)
    hop(0, 3)
    other(0, 1)
    own(0, 2)
    hop(1, 3)
    hop(0, 4)
    other(0, 2)
    own(0, 3)
    other(0, 3)
    own(0, 4)
    other(0, 4)
    project(0)
    early = gathers(0)
    for one in early:
        one.begin()
    own(1, 0)
    other(1, 0)
    own(1, 1)
    for one in early:
        one.near()
    hop(1, 4)
    other(1, 1)
    own(1, 2)
    other(1, 2)
    for one in early:
        one.far()
    own(1, 3)
    other(1, 3)
    own(1, 4)
    other(1, 4)
    project(1)
    late = gathers(1)
    for one in late:
        one.begin()
    for i in range(4):
        for one in early:
            one.relay(one.relays()[i])
    for one in late:
        one.near()
    for one in late:
        one.relay(one.relays()[0])
    for one in late:
        one.far()
    mine = pl.ds(pl.multiple_of(place.head * (rows // heads), rows // heads), rows // heads)
    for slot in range(heads):
        part_ref[slot] = st[slot, mine, :]
    for i in range(1, 4):
        for one in late:
            one.relay(one.relays()[i])
    for one in early + late:
        one.end()
    sender.finish()


def pool(states, key_weight, value_weight):
    rows, feats = states.shape
    cols = key_weight.shape[1]
    heads = key_weight.shape[0] // feats
    seqs = SIDE * SIDE
    vmem, anywhere = pl.BlockSpec(memory_space=pltpu.VMEM), pl.BlockSpec(memory_space=pl.ANY)
    dma = pltpu.SemaphoreType.DMA
    return pl.pallas_call(
        pool_kernel,
        out_shape=(
            jax.ShapeDtypeStruct((2, seqs, rows, cols), jnp.bfloat16),
            jax.ShapeDtypeStruct((heads, rows // heads, feats), jnp.bfloat16),
        ),
        in_specs=[vmem, anywhere, anywhere],
        out_specs=(vmem, vmem),
        scratch_shapes=[
            pltpu.VMEM((heads, rows, feats), jnp.bfloat16),
            pltpu.VMEM((2, heads, feats, cols), jnp.bfloat16),
            pltpu.VMEM((rows, 2 * cols), jnp.float32),
            dma((160,)),
            dma((heads, 2)),
            dma((heads, 2)),
            dma((2, seqs, 4)),
            dma((2,)),
        ],
        compiler_params=pltpu.CompilerParams(
            collective_id=1, has_side_effects=True, vmem_limit_bytes=40 * MIB
        ),
        name="pool",
    )(states, key_weight.reshape(heads, feats, cols), value_weight.reshape(heads, feats, cols))


def reduce_kernel(dkv_ref, all_ref, box, mid, box2, send_sems, box_recv, box2_recv, pool_recv):
    place = Place()
    rows = dkv_ref.shape[2]
    half = rows // 2
    halves = (pl.ds(0, half), pl.ds(half, half))
    offsets = (2, 1, 3, 0)
    greet([place.along(i, d) for i in (True, False) for d in (1, -1)])
    sender = Sender(send_sems)
    ways = ((0, 1), (1, -1))

    def add(*terms):
        total = terms[0].astype(jnp.float32)
        for term in terms[1:]:
            total = total + term.astype(jnp.float32)
        return total.astype(jnp.bfloat16)

    def send1(j, way, sign, kind, k, src):
        sender.send(src, box.at[j, way, kind, k], box_recv.at[j, way, kind, k], place.along(j == 0, sign))

    def wait1(j, way, kind, k):
        arrived(box.at[j, way, kind, k], send_sems.at[0], box_recv.at[j, way, kind, k], place.along(j == 0, 1))

    def send2(j, way, sign, kind, src):
        sender.send(src, box2.at[j, way, kind], box2_recv.at[j, way, kind], place.along(j != 0, sign))

    def wait2(j, way, kind):
        arrived(box2.at[j, way, kind], send_sems.at[0], box2_recv.at[j, way, kind], place.along(j != 0, 1))

    for k, second in enumerate(offsets):
        for j in range(2):
            for way, sign in ways:
                send1(j, way, sign, 0, k, dkv_ref.at[j, place.slot(j == 0, 2, second), halves[way], :])
    for k, second in enumerate(offsets):
        for j in range(2):
            for way, sign in ways:
                send1(j, way, sign, 1, k, dkv_ref.at[j, place.slot(j == 0, sign, second), halves[1 - way], :])
    for k, second in enumerate(offsets):
        for j in range(2):
            for way, sign in ways:
                wait1(j, way, 0, k)
                mine = dkv_ref[j, place.slot(j == 0, sign, second), halves[way], :]
                box[j, way, 0, k] = add(box[j, way, 0, k], mine)
                send1(j, way, sign, 2, k, box.at[j, way, 0, k])
    for k, second in enumerate(offsets):
        for j in range(2):
            for way, sign in ways:
                wait1(j, 1 - way, 1, k)
                wait1(j, way, 2, k)
                mine = dkv_ref[j, place.slot(j == 0, 0, second), halves[way], :]
                mid[j, k, halves[way], :] = add(mine, box[j, 1 - way, 1, k], box[j, way, 2, k])
            if k == 0:
                for way, sign in ways:
                    send2(j, way, sign, 0, mid.at[j, 0, halves[way], :])
            if k in (1, 2):
                way, sign = ways[k - 1]
                send2(j, way, sign, 1, mid.at[j, k, halves[1 - way], :])
    for j in range(2):
        for way, sign in ways:
            wait2(j, way, 0)
            box2[j, way, 0] = add(box2[j, way, 0], mid[j, 1 + way, halves[way], :])
            send2(j, way, sign, 2, box2.at[j, way, 0])
    gathers = []
    for way, sign in ways:
        for j in range(2):
            wait2(j, 1 - way, 1)
            wait2(j, way, 2)
            all_ref[j, place.seq, halves[way], :] = add(
                mid[j, 3, halves[way], :], box2[j, 1 - way, 1], box2[j, way, 2]
            )
            one = Gather(place, sender, all_ref, pool_recv, j, j != 0, way, way * half, half, sign)
            one.begin()
            gathers.append(one)
    for one in gathers:
        one.near()
    for one in gathers:
        one.relay(one.relays()[0])
    for one in gathers:
        one.far()
    for i in range(1, 4):
        for one in gathers:
            one.relay(one.relays()[i])
    for one in gathers:
        one.end()
    sender.finish()


def reduce_all(dkv):
    _, seqs, rows, cols = dkv.shape
    half = rows // 2
    vmem = pl.BlockSpec(memory_space=pltpu.VMEM)
    dma = pltpu.SemaphoreType.DMA
    return pl.pallas_call(
        reduce_kernel,
        out_shape=jax.ShapeDtypeStruct(dkv.shape, jnp.bfloat16),
        in_specs=[vmem],
        out_specs=vmem,
        scratch_shapes=[
            pltpu.VMEM((2, 2, 3, SIDE, half, cols), jnp.bfloat16),
            pltpu.VMEM((2, SIDE, rows, cols), jnp.bfloat16),
            pltpu.VMEM((2, 2, 3, half, cols), jnp.bfloat16),
            dma((128,)),
            dma((2, 2, 3, SIDE)),
            dma((2, 2, 3)),
            dma((2, seqs, 2)),
        ],
        compiler_params=pltpu.CompilerParams(
            collective_id=2, has_side_effects=True, vmem_limit_bytes=32 * MIB
        ),
        name="reduce_all",
    )(dkv)


def weight_kernel(t_ref, dkv_ref, dk_ref, dv_ref):
    heads, seqs, rows, feats = t_ref.shape
    dk_ref[...] = jnp.zeros_like(dk_ref)
    dv_ref[...] = jnp.zeros_like(dv_ref)

    def block(s, _):
        left = t_ref[:, pl.ds(s, 1), :, :].reshape(heads * rows, feats)
        dk_ref[...] += dot_tn(left, dkv_ref[0, s])
        dv_ref[...] += dot_tn(left, dkv_ref[1, s])
        return 0

    lax.fori_loop(0, seqs, block, 0)


def weight_grads(t, dkv):
    heads, seqs, rows, feats = t.shape
    cols = dkv.shape[3]
    vmem = pl.BlockSpec(memory_space=pltpu.VMEM)
    return pl.pallas_call(
        weight_kernel,
        out_shape=(jax.ShapeDtypeStruct((feats, cols), jnp.float32),) * 2,
        in_specs=[vmem, vmem],
        out_specs=(vmem, vmem),
        compiler_params=pltpu.CompilerParams(vmem_limit_bytes=24 * MIB),
        name="weight_grads",
    )(t, dkv)


def local(queries, states, key_weight, value_weight, neighbour_ids, out_grad):
    kv, part = pool(states, key_weight, value_weight)
    column = lax.all_to_all(part, "seq", split_axis=0, concat_axis=0, tiled=True)
    t = lax.all_gather(column, "head", axis=0, tiled=False)
    context, query_grad, dkv = attend(neighbour_ids, queries, out_grad, kv)
    dk, dv = weight_grads(t, reduce_all(dkv))
    return context, query_grad, dk, dv


def solution(mesh):
    in_specs = (
        P("seq", "head"),
        P("seq", "head"),
        P(None, "head"),
        P(None, "head"),
        P("seq", None),
        P("seq", "head"),
    )
    out_specs = (P("seq", "head"), P("seq", "head"), P("seq", "head"), P("seq", "head"))
    return jax.shard_map(local, mesh=mesh, in_specs=in_specs, out_specs=out_specs, check_vma=False)
```

```python
import math

import jax
import jax.numpy as jnp
from jax import lax
from jax.experimental import pallas as pl
from jax.experimental.pallas import tpu as pltpu
from jax.sharding import PartitionSpec as P

HD = 128
SPAN = 64
NBR = 128
TOPN = 2
SCALE = 1.0 / math.sqrt(HD)
MIB = 1 << 20
MESH = pl.DeviceIdType.MESH
SIDE = 4
RING = 8
BATCHES = 4
ORDER = (
    ("start", 0), ("start", 1), ("hop", 0, 1, 0, 1), ("hop", 0, 1, 0, -1), ("hop", 0, 1, 1, 1), ("hop", 0, 1, 1, -1),
    ("twin", 0, -1), ("twin", 0, 1), ("hop", 1, 1, 0, 1), ("hop", 1, 1, 0, -1), ("hop", 1, 1, 1, 1),
    ("hop", 1, 1, 1, -1), ("twin", 1, -1), ("twin", 1, 1), ("other", 0, -1), ("other", 0, 0), ("own", 0, -1),
    ("hop", 0, 2, 0, 1), ("hop", 0, 2, 0, -1), ("own", 0, 0), ("own", 0, 1), ("other", 0, 1), ("hop", 0, 2, 1, 1),
    ("hop", 0, 2, 1, -1), ("twin", 0, -2), ("twin", 0, 2), ("own", 0, -2), ("own", 0, 2), ("other", 1, 0),
    ("hop", 1, 2, 0, 1), ("hop", 1, 2, 0, -1), ("own", 1, -1), ("own", 1, 0), ("own", 1, 1), ("hop", 1, 2, 1, 1),
    ("hop", 1, 2, 1, -1), ("twin", 1, -2), ("twin", 1, 2), ("other", 0, -2), ("other", 0, 2), ("hop", 0, 3, 0, 1),
    ("hop", 0, 3, 0, -1), ("own", 1, -2), ("own", 1, 2), ("other", 1, -1), ("hop", 0, 3, 1, 1), ("hop", 0, 3, 1, -1),
    ("twin", 0, -3), ("twin", 0, 3), ("own", 0, -3), ("own", 0, 3), ("other", 1, 1), ("hop", 1, 3, 0, 1),
    ("hop", 1, 3, 0, -1), ("other", 1, -2), ("other", 1, 2), ("own", 2, 0), ("hop", 1, 3, 1, 1), ("twin", 1, -3),
    ("hop", 1, 3, 1, -1), ("twin", 1, 3), ("other", 0, -3), ("start", 2), ("other", 0, 3), ("hop", 0, 4, 0, 1),
    ("own", 1, -3), ("own", 1, 3), ("own", 3, 0), ("hop", 0, 4, 1, -1), ("twin", 0, 4), ("own", 0, 4),
    ("other", 1, -3), ("start", 3), ("hop", 1, 4, 0, 1), ("other", 1, 3), ("other", 2, 0), ("hop", 1, 4, 1, -1),
    ("twin", 1, 4), ("other", 0, 4), ("project", 0), ("hop", 2, 1, 0, 1), ("hop", 2, 1, 0, -1), ("own", 1, 4),
    ("hop", 2, 1, 1, 1), ("twin", 2, -1), ("own", 2, -1), ("other", 3, 0), ("hop", 2, 1, 1, -1), ("twin", 2, 1),
    ("other", 1, 4), ("hop", 3, 1, 0, 1), ("project", 1), ("hop", 3, 1, 0, -1), ("hop", 3, 1, 1, 1), ("twin", 3, -1),
    ("own", 2, 1), ("other", 2, -1), ("hop", 3, 1, 1, -1), ("twin", 3, 1), ("near1", 0, 0), ("near2", 0, 0),
    ("relay", 0, 0, 0), ("hop", 2, 2, 0, 1), ("other", 2, 1), ("hop", 2, 2, 0, -1), ("relay", 0, 1, 0),
    ("near2", 0, 1), ("near1", 0, 1), ("hop", 2, 2, 1, 1), ("twin", 2, -2), ("hop", 2, 2, 1, -1), ("twin", 2, 2),
    ("own", 2, -2), ("own", 2, 2), ("near1", 1, 0), ("hop", 3, 2, 0, 1), ("near2", 1, 0), ("hop", 3, 2, 0, -1),
    ("relay", 1, 0, 0), ("own", 3, -1), ("own", 3, 1), ("hop", 3, 2, 1, 1), ("twin", 3, -2), ("relay", 1, 1, 0),
    ("hop", 3, 2, 1, -1), ("twin", 3, 2), ("near2", 1, 1), ("near1", 1, 1), ("far", 0, 0), ("hop", 2, 3, 0, 1),
    ("relay", 0, 0, 1), ("other", 2, -2), ("hop", 2, 3, 0, -1), ("other", 2, 2), ("own", 3, -2), ("hop", 2, 3, 1, 1),
    ("twin", 2, -3), ("relay", 0, 0, 2), ("hop", 2, 3, 1, -1), ("twin", 2, 3), ("relay", 0, 1, 2), ("own", 2, -3),
    ("own", 2, 3), ("hop", 3, 3, 0, 1), ("far", 0, 1), ("hop", 3, 3, 0, -1), ("relay", 0, 1, 1), ("own", 3, 2),
    ("other", 3, -1), ("hop", 3, 3, 1, 1), ("twin", 3, -3), ("relay", 1, 0, 1), ("other", 2, -3),
    ("hop", 3, 3, 1, -1), ("twin", 3, 3), ("far", 1, 0), ("relay", 1, 0, 2), ("hop", 2, 4, 0, 1), ("relay", 1, 1, 2),
    ("other", 2, 3), ("own", 3, -3), ("own", 3, 3), ("other", 3, 1), ("hop", 2, 4, 1, -1), ("twin", 2, 4),
    ("far", 1, 1), ("relay", 1, 1, 1), ("own", 2, 4), ("other", 3, -2), ("hop", 3, 4, 0, 1), ("relay", 0, 0, 3),
    ("other", 3, 2), ("other", 3, -3), ("other", 3, 3), ("other", 2, 4), ("hop", 3, 4, 1, -1), ("twin", 3, 4),
    ("project", 2), ("relay", 0, 1, 3), ("relay", 1, 0, 3), ("own", 3, 4), ("relay", 1, 1, 3), ("other", 3, 4),
    ("project", 3), ("swap", 0), ("near1", 2, 0), ("near2", 2, 0), ("relay", 2, 0, 0), ("relay", 2, 1, 0),
    ("near2", 2, 1), ("near1", 2, 1), ("near2", 3, 0), ("near1", 3, 0), ("relay", 3, 0, 0), ("near1", 3, 1),
    ("relay", 3, 1, 0), ("near2", 3, 1), ("swap", 1), ("relay", 2, 0, 1), ("far", 2, 0), ("relay", 2, 0, 2),
    ("relay", 2, 1, 2), ("relay", 2, 1, 1), ("far", 2, 1), ("relay", 3, 1, 1), ("far", 3, 0), ("relay", 3, 0, 2),
    ("relay", 3, 0, 1), ("far", 3, 1), ("relay", 3, 1, 2), ("relay", 2, 0, 3), ("relay", 3, 0, 3), ("relay", 2, 1, 3),
    ("relay", 3, 1, 3),
)


def dot_nt(a, b):
    return lax.dot_general(a, b, (((1,), (1,)), ((), ())), preferred_element_type=jnp.float32)


def dot_tn(a, b):
    return lax.dot_general(a, b, (((0,), (0,)), ((), ())), preferred_element_type=jnp.float32)


def dot_nn(a, b):
    return jnp.dot(a, b, preferred_element_type=jnp.float32)


def attend_kernel(ids_ref, q_ref, g_ref, kv_ref, ctx_ref, dq_ref, dkv_ref, acc_ref):
    cols = q_ref.shape[1]
    spans = q_ref.shape[0] // SPAN
    blocks = kv_ref.shape[1]
    first = lax.broadcasted_iota(jnp.int32, (SPAN, cols), 1) < HD

    def clear(i, _):
        for j in range(2):
            acc_ref[j, i] = jnp.zeros((NBR, cols), jnp.float32)
        return 0

    lax.fori_loop(0, blocks, clear, 0)

    def stack(x):
        zero = jnp.zeros_like(x)
        return jnp.concatenate([jnp.where(first, x, zero), jnp.where(first, zero, x)], axis=0)

    def unstack(x):
        return jnp.where(first, x[:SPAN], x[SPAN:])

    def span(c, _):
        rows = pl.ds(c * SPAN, SPAN)
        id0, id1 = ids_ref[c, 0], ids_ref[c, 1]
        keys = jnp.concatenate([kv_ref[0, id0], kv_ref[0, id1]], axis=0)
        values = jnp.concatenate([kv_ref[1, id0], kv_ref[1, id1]], axis=0)
        q2 = stack(q_ref[rows, :])
        g2 = stack(g_ref[rows, :])
        scores = dot_nt(q2, keys) * SCALE
        prob_grad = dot_nt(g2, values)
        top = jnp.max(scores, axis=-1, keepdims=True)
        e = jnp.exp(scores - top)
        probs = e / jnp.sum(e, axis=-1, keepdims=True)
        low = probs.astype(jnp.bfloat16)
        delta = jnp.sum(probs * prob_grad, axis=-1, keepdims=True)
        sg = (probs * (prob_grad - delta) * SCALE).astype(jnp.bfloat16)
        ctx_ref[rows, :] = unstack(dot_nn(low, values)).astype(jnp.bfloat16)
        dq_ref[rows, :] = unstack(dot_nn(sg, keys)).astype(jnp.bfloat16)
        dk = dot_tn(sg, q2)
        dv = dot_tn(low, g2)
        acc_ref[0, id0] += dk[:NBR]
        acc_ref[1, id0] += dv[:NBR]
        acc_ref[0, id1] += dk[NBR:]
        acc_ref[1, id1] += dv[NBR:]
        return 0

    lax.fori_loop(0, spans, span, 0)

    def store(i, _):
        for j in range(2):
            dkv_ref[j, i] = acc_ref[j, i].astype(jnp.bfloat16)
        return 0

    lax.fori_loop(0, blocks, store, 0)


def attend(ids, queries, grads, kv):
    rows, cols = queries.shape
    blocks = kv.shape[1] * kv.shape[2] // NBR
    vmem = pl.BlockSpec(memory_space=pltpu.VMEM)
    context, query_grad, dkv = pl.pallas_call(
        attend_kernel,
        out_shape=(
            jax.ShapeDtypeStruct((rows, cols), jnp.bfloat16),
            jax.ShapeDtypeStruct((rows, cols), jnp.bfloat16),
            jax.ShapeDtypeStruct((2, blocks, NBR, cols), jnp.bfloat16),
        ),
        in_specs=[pl.BlockSpec(memory_space=pltpu.SMEM), vmem, vmem, vmem],
        out_specs=(vmem, vmem, vmem),
        scratch_shapes=[pltpu.VMEM((2, blocks, NBR, cols), jnp.float32)],
        compiler_params=pltpu.CompilerParams(vmem_limit_bytes=40 * MIB),
        name="attend",
    )(ids, queries, grads, kv.reshape(2, blocks, NBR, cols))
    return context, query_grad, dkv.reshape(kv.shape)


class Place:
    def __init__(self):
        self.seq = lax.axis_index("seq")
        self.head = lax.axis_index("head")
        x, z = lax.div(self.seq, SIDE), lax.div(self.head, 2)
        y, self.core = self.seq - x * SIDE, self.head - z * 2
        self.xs = [x] + [lax.rem(x + i, SIDE) for i in range(1, SIDE)]
        self.ys = [y] + [lax.rem(y + i, SIDE) for i in range(1, SIDE)]
        self.zs = [z] + [lax.rem(z + i, RING) for i in range(1, RING)]
        self.pairs = [2 * z for z in self.zs]
        self.rows = [SIDE * x for x in self.xs]
        self.other = (self.seq, self.pairs[0] + 1 - self.core)

    def along(self, is_x, step):
        return (self.slot(is_x, step, 0), self.head)

    def ring(self, step):
        return (self.seq, self.pairs[step % RING] + self.core)

    def twin(self):
        return self.other

    def slot(self, first_is_x, first, second):
        if not first_is_x:
            first, second = second, first
        return self.rows[first % SIDE] + self.ys[second % SIDE]


def greet(devices):
    barrier = pltpu.get_barrier_semaphore()
    for device in devices:
        pl.semaphore_signal(barrier, inc=1, device_id=device, device_id_type=MESH)
    pl.semaphore_wait(barrier, len(devices))


class Sender:
    def __init__(self, sems):
        self.sems, self.started = sems, []

    def send(self, src, dst, recv_sem, device):
        copy = pltpu.make_async_remote_copy(
            src_ref=src,
            dst_ref=dst,
            send_sem=self.sems.at[len(self.started)],
            recv_sem=recv_sem,
            device_id=device,
            device_id_type=MESH,
        )
        copy.start()
        self.started.append(copy)

    def finish(self):
        for copy in self.started:
            copy.wait_send()


def arrived(ref, send_sem, recv_sem, device):
    pltpu.make_async_remote_copy(
        src_ref=ref, dst_ref=ref, send_sem=send_sem, recv_sem=recv_sem, device_id=device, device_id_type=MESH
    ).wait_recv()


class Gather:
    def __init__(self, place, sender, buf, recv, j, first_is_x, cid, row, rows, sign):
        self.place, self.sender, self.buf, self.recv = place, sender, buf, recv
        self.j, self.fx, self.cid, self.row, self.rows, self.sign = j, first_is_x, cid, row, rows, sign

    def ref(self, slot):
        return self.buf.at[self.j, slot, pl.ds(self.row, self.rows), :]

    def send(self, offsets, is_x, step):
        slot = self.place.slot(self.fx, *offsets)
        self.sender.send(
            self.ref(slot), self.ref(slot), self.recv.at[self.j, slot, self.cid], self.place.along(is_x, step)
        )

    def wait(self, offsets):
        slot = self.place.slot(self.fx, *offsets)
        arrived(self.ref(slot), self.sender.sems.at[0], self.recv.at[self.j, slot, self.cid], self.place.twin())

    def spread(self, first):
        self.send((first, 0), not self.fx, self.sign)
        self.send((first, 0), not self.fx, -self.sign)

    def begin(self):
        self.send((0, 0), self.fx, self.sign)
        self.send((0, 0), self.fx, -self.sign)
        self.spread(0)

    def near(self, which):
        if which == 1:
            self.wait((-self.sign, 0))
            self.send((-self.sign, 0), self.fx, self.sign)
            self.spread(-self.sign)
        else:
            self.wait((self.sign, 0))
            self.spread(self.sign)

    def far(self):
        self.wait((-2 * self.sign, 0))
        self.spread(2)

    def relay(self, first):
        self.wait((first, -self.sign))
        self.send((first, -self.sign), not self.fx, self.sign)

    def relays(self):
        return [0, -self.sign, self.sign, 2]

    def end(self):
        for first in self.relays():
            self.wait((first, self.sign))
            self.wait((first, 2))


class Ring:
    def __init__(self, place, sender, at, ring_recv, twin_recv, rows):
        self.place, self.sender, self.at = place, sender, at
        self.ring_recv, self.twin_recv, self.rows = ring_recv, twin_recv, rows

    def slot(self, distance, other):
        core = 1 - self.place.core if other else self.place.core
        return self.place.pairs[distance % RING] + core

    def unit(self, slot, b, u):
        half = self.rows // 2
        return self.at(slot, b * self.rows + u * half, half)

    def batch(self, slot, b):
        return self.at(slot, b * self.rows, self.rows)

    def signs(self, d, u):
        return (1, -1) if d < RING // 2 else ((1,) if u == 0 else (-1,))

    def to_ring(self, slot, b, u, sign):
        ref = self.unit(slot, b, u)
        self.sender.send(ref, ref, self.ring_recv.at[slot, 2 * b + u], self.place.ring(sign))

    def to_twin(self, slot, b):
        ref = self.batch(slot, b)
        self.sender.send(ref, ref, self.twin_recv.at[slot, b], self.place.twin())

    def start(self, b):
        for u in range(2):
            for sign in (1, -1):
                self.to_ring(self.place.head, b, u, sign)
        self.to_twin(self.place.head, b)

    def distances(self, d):
        return (0,) if d == 0 else ((-d, d) if d < RING // 2 else (d,))

    def relay(self, b, d, u, sign):
        slot = self.slot(-sign * d, False)
        arrived(self.unit(slot, b, u), self.sender.sems.at[0], self.ring_recv.at[slot, 2 * b + u], self.place.twin())
        if d < RING // 2 and sign in self.signs(d + 1, u):
            self.to_ring(slot, b, u, sign)

    def hop(self, b, d):
        for u in range(2):
            for sign in self.signs(d, u):
                self.relay(b, d, u, sign)
        for distance in self.distances(d):
            self.to_twin(self.slot(distance, False), b)

    def from_twin(self, b, distance):
        slot = self.slot(distance, True)
        arrived(self.batch(slot, b), self.sender.sems.at[0], self.twin_recv.at[slot, b], self.place.twin())


def pool_kernel(
    states_ref, kw_ref, vw_ref, kv_ref, part_ref, st, shares, mid, w, acc,
    send_sems, twin_recv, ring_recv, pool_recv, swap_recv, w_sems,
):
    place = Place()
    rows, feats = st.shape[1:]
    cols = kv_ref.shape[3]
    batches = BATCHES
    batch = rows // batches
    loads = [pltpu.make_async_copy(kw_ref, w.at[0], w_sems.at[0]), pltpu.make_async_copy(vw_ref, w.at[1], w_sems.at[1])]
    for load in loads:
        load.start()
    st[place.head] = states_ref[...]
    acc[...] = jnp.zeros_like(acc)
    greet(
        [place.ring(1), place.ring(-1), place.twin()]
        + [place.along(i, d) for i in (True, False) for d in (1, -1, 2)]
    )
    sender = Sender(send_sems)

    def at(slot, row, n):
        return st.at[slot, pl.ds(row, n), :]

    ring = Ring(place, sender, at, ring_recv, twin_recv, batch)

    def multiply(slot, b):
        here = pl.ds(b * batch, batch)
        left = st[slot, here, :]
        acc[here, :cols] += dot_nn(left, w[0, slot])
        acc[here, cols:] += dot_nn(left, w[1, slot])

    def own(b, distance):
        multiply(ring.slot(distance, False), b)

    def other(b, distance):
        ring.from_twin(b, distance)
        multiply(ring.slot(distance, True), b)

    def twin(b, distance):
        ring.to_twin(ring.slot(distance, False), b)

    def project(b):
        here = pl.ds(b * batch, batch)
        kv_ref[0, place.seq, here, :] = acc[here, :cols].astype(kv_ref.dtype)
        kv_ref[1, place.seq, here, :] = acc[here, cols:].astype(kv_ref.dtype)
        for one in gathers[b]:
            one.begin()

    gathers = [
        [
            Gather(place, sender, kv_ref, pool_recv, j, j == 0, b, b * batch, batch, 1 if (b + j) % 2 == 0 else -1)
            for j in range(2)
        ]
        for b in range(batches)
    ]

    share = rows // (SIDE * SIDE)
    mine = pl.ds(pl.multiple_of(place.head * share, share), share)
    side = [pl.ds(0, feats // 2), pl.ds(feats // 2, feats // 2)]
    here = (place.xs, place.ys)
    steps = (2, 1, -1)

    def gather_share():
        for slot in range(SIDE * SIDE):
            x, y = slot // SIDE, slot % SIDE
            shares[0, x, y] = st[slot, mine, side[0]]
            shares[1, y, x] = st[slot, mine, side[1]]

    def column(j, source):
        return part_ref.at[:, source, :, side[j]] if j == 0 else part_ref.at[source, :, :, side[j]]

    def swap_first():
        gather_share()
        for i, step in enumerate(steps):
            for j in range(2):
                sender.send(
                    shares.at[j, here[j][step % SIDE]], mid.at[j, here[j][0]], swap_recv.at[j, 0, i],
                    place.along(j == 0, step),
                )
        for j in range(2):
            mid[j, here[j][0]] = shares[j, here[j][0]]

    def swap_second():
        for i, step in enumerate(steps):
            for j in range(2):
                arrived(mid.at[j, here[j][-step % SIDE]], send_sems.at[0], swap_recv.at[j, 0, i], place.twin())
        for i, step in enumerate(steps):
            for j in range(2):
                sender.send(
                    mid.at[j, :, here[1 - j][step % SIDE]], column(j, here[1 - j][0]), swap_recv.at[j, 1, i],
                    place.along(j != 0, step),
                )
        for j in range(2):
            column(j, here[1 - j][0])[...] = mid[j, :, here[1 - j][0]]

    def swap_end():
        for i, step in enumerate(steps):
            for j in range(2):
                arrived(column(j, here[1 - j][-step % SIDE]), send_sems.at[0], swap_recv.at[j, 1, i], place.twin())

    steps_of = {
        "start": ring.start,
        "hop": ring.relay,
        "twin": twin,
        "own": own,
        "other": other,
        "project": project,
        "near1": lambda b, j: gathers[b][j].near(1),
        "near2": lambda b, j: gathers[b][j].near(2),
        "far": lambda b, j: gathers[b][j].far(),
        "relay": lambda b, j, i: gathers[b][j].relay(gathers[b][j].relays()[i]),
        "swap": lambda i: (swap_first, swap_second)[i](),
    }
    waiting = list(loads)
    for name, *what in ORDER:
        if name in ("own", "other") and waiting:
            for load in waiting:
                load.wait()
            waiting = []
        steps_of[name](*what)
    swap_end()
    for b in range(batches):
        for one in gathers[b]:
            one.end()
    sender.finish()


def pool(states, key_weight, value_weight):
    rows, feats = states.shape
    cols = key_weight.shape[1]
    heads = key_weight.shape[0] // feats
    seqs = SIDE * SIDE
    share = rows // heads
    vmem, hbm = pl.BlockSpec(memory_space=pltpu.VMEM), pl.BlockSpec(memory_space=pltpu.HBM)
    dma = pltpu.SemaphoreType.DMA
    return pl.pallas_call(
        pool_kernel,
        out_shape=(
            jax.ShapeDtypeStruct((2, seqs, rows, cols), jnp.bfloat16),
            jax.ShapeDtypeStruct((SIDE, SIDE, share, feats), jnp.bfloat16),
        ),
        in_specs=[vmem, hbm, hbm],
        out_specs=(vmem, vmem),
        scratch_shapes=[
            pltpu.VMEM((heads, rows, feats), jnp.bfloat16),
            pltpu.VMEM((2, SIDE, SIDE, share, feats // 2), jnp.bfloat16),
            pltpu.VMEM((2, SIDE, SIDE, share, feats // 2), jnp.bfloat16),
            pltpu.VMEM((2, heads, feats, cols), jnp.bfloat16),
            pltpu.VMEM((rows, 2 * cols), jnp.float32),
            dma((256,)),
            dma((heads, BATCHES)),
            dma((heads, 2 * BATCHES)),
            dma((2, seqs, BATCHES)),
            dma((2, 2, 3)),
            dma((2,)),
        ],
        compiler_params=pltpu.CompilerParams(
            collective_id=1, has_side_effects=True, vmem_limit_bytes=56 * MIB
        ),
        name="pool",
    )(states, key_weight.reshape(heads, feats, cols), value_weight.reshape(heads, feats, cols))


def reduce_kernel(
    dkv_ref, part_ref, dk_ref, dv_ref, pooled, t, box, mid, box2,
    send_sems, box_recv, box2_recv, pool_recv, twin_recv, ring_recv,
):
    place = Place()
    rows, cols = dkv_ref.shape[2], dkv_ref.shape[3]
    heads, feats = t.shape[0], t.shape[2]
    share = rows // heads
    half = rows // 2
    halves = (pl.ds(0, half), pl.ds(half, half))
    offsets = (2, 1, 3, 0)
    t[place.head] = part_ref[...]
    greet(
        [place.along(i, d) for i in (True, False) for d in (1, -1)] + [place.ring(1), place.ring(-1), place.twin()]
    )
    sender = Sender(send_sems)
    ways = ((0, 1), (1, -1))
    ring = Ring(place, sender, lambda slot, row, n: t.at[slot, pl.ds(row, n), :], ring_recv, twin_recv, rows)

    def add(*terms):
        total = terms[0].astype(jnp.float32)
        for term in terms[1:]:
            total = total + term.astype(jnp.float32)
        return total.astype(jnp.bfloat16)

    def send1(j, way, sign, kind, k, src):
        sender.send(src, box.at[j, way, kind, k], box_recv.at[j, way, kind, k], place.along(j == 0, sign))

    def wait1(j, way, kind, k):
        arrived(box.at[j, way, kind, k], send_sems.at[0], box_recv.at[j, way, kind, k], place.along(j == 0, 1))

    def send2(j, way, sign, kind, src):
        sender.send(src, box2.at[j, way, kind], box2_recv.at[j, way, kind], place.along(j != 0, sign))

    def wait2(j, way, kind):
        arrived(box2.at[j, way, kind], send_sems.at[0], box2_recv.at[j, way, kind], place.along(j != 0, 1))

    for k, second in enumerate(offsets):
        for j in range(2):
            for way, sign in ways:
                send1(j, way, sign, 0, k, dkv_ref.at[j, place.slot(j == 0, 2, second), halves[way], :])
    for k, second in enumerate(offsets):
        for j in range(2):
            for way, sign in ways:
                send1(j, way, sign, 1, k, dkv_ref.at[j, place.slot(j == 0, sign, second), halves[1 - way], :])
    ring.start(0)
    for k, second in enumerate(offsets):
        for j in range(2):
            for way, sign in ways:
                wait1(j, way, 0, k)
                mine = dkv_ref[j, place.slot(j == 0, sign, second), halves[way], :]
                box[j, way, 0, k] = add(box[j, way, 0, k], mine)
                send1(j, way, sign, 2, k, box.at[j, way, 0, k])
    dk_ref[...] = jnp.zeros_like(dk_ref)
    dv_ref[...] = jnp.zeros_like(dv_ref)
    ring.hop(0, 1)
    for k, second in enumerate(offsets):
        for j in range(2):
            for way, sign in ways:
                wait1(j, 1 - way, 1, k)
                wait1(j, way, 2, k)
                mine = dkv_ref[j, place.slot(j == 0, 0, second), halves[way], :]
                mid[j, k, halves[way], :] = add(mine, box[j, 1 - way, 1, k], box[j, way, 2, k])
            if k == 0:
                for way, sign in ways:
                    send2(j, way, sign, 0, mid.at[j, 0, halves[way], :])
            if k in (1, 2):
                way, sign = ways[k - 1]
                send2(j, way, sign, 1, mid.at[j, k, halves[1 - way], :])
        if k == 1:
            ring.hop(0, 2)
    for j in range(2):
        for way, sign in ways:
            wait2(j, way, 0)
            box2[j, way, 0] = add(box2[j, way, 0], mid[j, 1 + way, halves[way], :])
            send2(j, way, sign, 2, box2.at[j, way, 0])
    ring.hop(0, 3)
    gathers = []
    for way, sign in ways:
        for j in range(2):
            wait2(j, 1 - way, 1)
            wait2(j, way, 2)
            pooled[j, place.seq, halves[way], :] = add(
                mid[j, 3, halves[way], :], box2[j, 1 - way, 1], box2[j, way, 2]
            )
            one = Gather(place, sender, pooled, pool_recv, j, j != 0, way, way * half, half, sign)
            one.begin()
            gathers.append(one)

    def near():
        for which in (1, 2):
            for one in gathers:
                one.near(which)

    def far():
        for one in gathers:
            one.far()

    def relay(i):
        for one in gathers:
            one.relay(one.relays()[i])

    def rest(i, second):
        for one in gathers:
            one.wait((one.relays()[i], one.sign * second))

    def multiply(x, y):
        slot = place.slot(True, x, y)
        left = t[:, pl.ds(pl.multiple_of(slot * share, share), share), :].reshape(rows, feats)
        right = jnp.concatenate([pooled[0, slot], pooled[1, slot]], axis=1)
        product = dot_tn(left, right)
        dk_ref[...] += product[:, :cols]
        dv_ref[...] += product[:, cols:]

    near()
    ring.hop(0, 4)
    relay(0)
    for distance in range(-RING // 2 + 1, RING // 2 + 1):
        ring.from_twin(0, distance)
    multiply(0, 0)
    far()
    relay(1)
    relay(2)
    rest(0, 1)
    for step in (1, -1):
        multiply(step, 0)
        multiply(0, step)
    relay(3)
    rest(0, 2)
    multiply(2, 0)
    multiply(0, 2)
    rest(1, 1)
    rest(2, 1)
    for x in (1, -1):
        for y in (1, -1):
            multiply(x, y)
    rest(1, 2)
    rest(2, 2)
    rest(3, 1)
    for step in (1, -1):
        multiply(step, 2)
        multiply(2, step)
    rest(3, 2)
    multiply(2, 2)
    sender.finish()


def weight_grads(dkv, part):
    _, seqs, rows, cols = dkv.shape
    feats = part.shape[1]
    heads = 2 * RING
    half = rows // 2
    vmem = pl.BlockSpec(memory_space=pltpu.VMEM)
    dma = pltpu.SemaphoreType.DMA
    return pl.pallas_call(
        reduce_kernel,
        out_shape=(jax.ShapeDtypeStruct((feats, cols), jnp.float32),) * 2,
        in_specs=[vmem, vmem],
        out_specs=(vmem, vmem),
        scratch_shapes=[
            pltpu.VMEM((2, seqs, rows, cols), jnp.bfloat16),
            pltpu.VMEM((heads, rows, feats), jnp.bfloat16),
            pltpu.VMEM((2, 2, 3, SIDE, half, cols), jnp.bfloat16),
            pltpu.VMEM((2, SIDE, rows, cols), jnp.bfloat16),
            pltpu.VMEM((2, 2, 3, half, cols), jnp.bfloat16),
            dma((192,)),
            dma((2, 2, 3, SIDE)),
            dma((2, 2, 3)),
            dma((2, seqs, 2)),
            dma((heads, 1)),
            dma((heads, 2)),
        ],
        compiler_params=pltpu.CompilerParams(
            collective_id=2, has_side_effects=True, vmem_limit_bytes=32 * MIB
        ),
        name="reduce_all",
    )(dkv, part)


def local(queries, states, key_weight, value_weight, neighbour_ids, out_grad):
    kv, part = pool(states, key_weight, value_weight)
    context, query_grad, dkv = attend(neighbour_ids, queries, out_grad, kv)
    dk, dv = weight_grads(dkv, part.reshape(states.shape))
    return context, query_grad, dk, dv


def solution(mesh):
    in_specs = (
        P("seq", "head"),
        P("seq", "head"),
        P(None, "head"),
        P(None, "head"),
        P("seq", None),
        P("seq", "head"),
    )
    out_specs = (P("seq", "head"), P("seq", "head"), P("seq", "head"), P("seq", "head"))
    return jax.shard_map(local, mesh=mesh, in_specs=in_specs, out_specs=out_specs, check_vma=False)
```

```python
import math

import jax
import jax.numpy as jnp
from jax import lax
from jax.experimental import pallas as pl
from jax.experimental.pallas import tpu as pltpu
from jax.sharding import PartitionSpec as P

HD = 128
SPAN = 64
NBR = 128
TOPN = 2
SCALE = 1.0 / math.sqrt(HD)
MIB = 1 << 20
MESH = pl.DeviceIdType.MESH
SIDE = 4
RING = 8
BATCHES = 4
ORDER = (
    ("start", 0), ("start", 1), ("hop", 0, 1, 0, 1), ("hop", 0, 1, 0, -1), ("hop", 0, 1, 1, 1), ("hop", 0, 1, 1, -1),
    ("twin", 0, -1), ("twin", 0, 1), ("hop", 1, 1, 0, 1), ("hop", 1, 1, 0, -1), ("hop", 1, 1, 1, 1),
    ("hop", 1, 1, 1, -1), ("twin", 1, -1), ("twin", 1, 1), ("other", 0, -1), ("other", 0, 0), ("own", 0, -1),
    ("hop", 0, 2, 0, 1), ("hop", 0, 2, 0, -1), ("own", 0, 0), ("own", 0, 1), ("other", 0, 1), ("hop", 0, 2, 1, 1),
    ("hop", 0, 2, 1, -1), ("twin", 0, -2), ("twin", 0, 2), ("own", 0, -2), ("own", 0, 2), ("other", 1, 0),
    ("hop", 1, 2, 0, 1), ("hop", 1, 2, 0, -1), ("own", 1, -1), ("own", 1, 0), ("own", 1, 1), ("hop", 1, 2, 1, 1),
    ("hop", 1, 2, 1, -1), ("twin", 1, -2), ("twin", 1, 2), ("other", 0, -2), ("other", 0, 2), ("hop", 0, 3, 0, 1),
    ("hop", 0, 3, 0, -1), ("own", 1, -2), ("own", 1, 2), ("other", 1, -1), ("hop", 0, 3, 1, 1), ("hop", 0, 3, 1, -1),
    ("twin", 0, -3), ("twin", 0, 3), ("own", 0, -3), ("own", 0, 3), ("other", 1, 1), ("hop", 1, 3, 0, 1),
    ("hop", 1, 3, 0, -1), ("other", 1, -2), ("other", 1, 2), ("own", 2, 0), ("hop", 1, 3, 1, 1), ("twin", 1, -3),
    ("hop", 1, 3, 1, -1), ("twin", 1, 3), ("other", 0, -3), ("start", 2), ("other", 0, 3), ("hop", 0, 4, 0, 1),
    ("own", 1, -3), ("own", 1, 3), ("own", 3, 0), ("hop", 0, 4, 1, -1), ("twin", 0, 4), ("own", 0, 4),
    ("other", 1, -3), ("start", 3), ("hop", 1, 4, 0, 1), ("other", 1, 3), ("other", 2, 0), ("hop", 1, 4, 1, -1),
    ("twin", 1, 4), ("other", 0, 4), ("project", 0), ("hop", 2, 1, 0, 1), ("hop", 2, 1, 0, -1), ("own", 1, 4),
    ("hop", 2, 1, 1, 1), ("twin", 2, -1), ("own", 2, -1), ("other", 3, 0), ("hop", 2, 1, 1, -1), ("twin", 2, 1),
    ("other", 1, 4), ("hop", 3, 1, 0, 1), ("project", 1), ("hop", 3, 1, 0, -1), ("hop", 3, 1, 1, 1), ("twin", 3, -1),
    ("own", 2, 1), ("other", 2, -1), ("hop", 3, 1, 1, -1), ("twin", 3, 1), ("near1", 0, 0), ("near2", 0, 0),
    ("relay", 0, 0, 0), ("hop", 2, 2, 0, 1), ("other", 2, 1), ("hop", 2, 2, 0, -1), ("relay", 0, 1, 0),
    ("near2", 0, 1), ("near1", 0, 1), ("hop", 2, 2, 1, 1), ("twin", 2, -2), ("hop", 2, 2, 1, -1), ("twin", 2, 2),
    ("own", 2, -2), ("own", 2, 2), ("near1", 1, 0), ("hop", 3, 2, 0, 1), ("near2", 1, 0), ("hop", 3, 2, 0, -1),
    ("relay", 1, 0, 0), ("own", 3, -1), ("own", 3, 1), ("hop", 3, 2, 1, 1), ("twin", 3, -2), ("relay", 1, 1, 0),
    ("hop", 3, 2, 1, -1), ("twin", 3, 2), ("near2", 1, 1), ("near1", 1, 1), ("far", 0, 0), ("hop", 2, 3, 0, 1),
    ("relay", 0, 0, 1), ("other", 2, -2), ("hop", 2, 3, 0, -1), ("other", 2, 2), ("own", 3, -2), ("hop", 2, 3, 1, 1),
    ("twin", 2, -3), ("relay", 0, 0, 2), ("hop", 2, 3, 1, -1), ("twin", 2, 3), ("relay", 0, 1, 2), ("own", 2, -3),
    ("own", 2, 3), ("hop", 3, 3, 0, 1), ("far", 0, 1), ("hop", 3, 3, 0, -1), ("relay", 0, 1, 1), ("own", 3, 2),
    ("other", 3, -1), ("hop", 3, 3, 1, 1), ("twin", 3, -3), ("relay", 1, 0, 1), ("other", 2, -3),
    ("hop", 3, 3, 1, -1), ("twin", 3, 3), ("far", 1, 0), ("relay", 1, 0, 2), ("hop", 2, 4, 0, 1), ("relay", 1, 1, 2),
    ("other", 2, 3), ("own", 3, -3), ("own", 3, 3), ("other", 3, 1), ("hop", 2, 4, 1, -1), ("twin", 2, 4),
    ("far", 1, 1), ("relay", 1, 1, 1), ("own", 2, 4), ("other", 3, -2), ("hop", 3, 4, 0, 1), ("relay", 0, 0, 3),
    ("other", 3, 2), ("other", 3, -3), ("other", 3, 3), ("other", 2, 4), ("hop", 3, 4, 1, -1), ("twin", 3, 4),
    ("project", 2), ("relay", 0, 1, 3), ("relay", 1, 0, 3), ("own", 3, 4), ("relay", 1, 1, 3), ("other", 3, 4),
    ("project", 3), ("swap", 0), ("near1", 2, 0), ("near2", 2, 0), ("relay", 2, 0, 0), ("relay", 2, 1, 0),
    ("near2", 2, 1), ("near1", 2, 1), ("near2", 3, 0), ("near1", 3, 0), ("relay", 3, 0, 0), ("near1", 3, 1),
    ("relay", 3, 1, 0), ("near2", 3, 1), ("swap", 1), ("relay", 2, 0, 1), ("far", 2, 0), ("relay", 2, 0, 2),
    ("relay", 2, 1, 2), ("relay", 2, 1, 1), ("far", 2, 1), ("relay", 3, 1, 1), ("far", 3, 0), ("relay", 3, 0, 2),
    ("relay", 3, 0, 1), ("far", 3, 1), ("relay", 3, 1, 2), ("relay", 2, 0, 3), ("relay", 3, 0, 3), ("relay", 2, 1, 3),
    ("relay", 3, 1, 3),
)


def dot_nt(a, b):
    return lax.dot_general(a, b, (((1,), (1,)), ((), ())), preferred_element_type=jnp.float32)


def dot_tn(a, b):
    return lax.dot_general(a, b, (((0,), (0,)), ((), ())), preferred_element_type=jnp.float32)


def dot_nn(a, b):
    return jnp.dot(a, b, preferred_element_type=jnp.float32)


def attend_kernel(ids_ref, q_ref, g_ref, kv_ref, ctx_ref, dq_ref, dkv_ref, acc_ref):
    cols = q_ref.shape[1]
    spans = q_ref.shape[0] // SPAN
    blocks = kv_ref.shape[1]
    first = lax.broadcasted_iota(jnp.int32, (SPAN, cols), 1) < HD

    def clear(i, _):
        for j in range(2):
            acc_ref[j, i] = jnp.zeros((NBR, cols), jnp.float32)
        return 0

    lax.fori_loop(0, blocks, clear, 0)

    def stack(x):
        zero = jnp.zeros_like(x)
        return jnp.concatenate([jnp.where(first, x, zero), jnp.where(first, zero, x)], axis=0)

    def unstack(x):
        return jnp.where(first, x[:SPAN], x[SPAN:])

    def span(c, _):
        rows = pl.ds(c * SPAN, SPAN)
        id0, id1 = ids_ref[0, c], ids_ref[1, c]
        keys = jnp.concatenate([kv_ref[0, id0], kv_ref[0, id1]], axis=0)
        values = jnp.concatenate([kv_ref[1, id0], kv_ref[1, id1]], axis=0)
        q2 = stack(q_ref[rows, :])
        g2 = stack(g_ref[rows, :])
        scores = dot_nt(q2, keys) * SCALE
        prob_grad = dot_nt(g2, values)
        top = jnp.max(scores, axis=-1, keepdims=True)
        e = jnp.exp(scores - top)
        probs = e / jnp.sum(e, axis=-1, keepdims=True)
        low = probs.astype(jnp.bfloat16)
        delta = jnp.sum(probs * prob_grad, axis=-1, keepdims=True)
        sg = (probs * (prob_grad - delta) * SCALE).astype(jnp.bfloat16)
        ctx_ref[rows, :] = unstack(dot_nn(low, values)).astype(jnp.bfloat16)
        dq_ref[rows, :] = unstack(dot_nn(sg, keys)).astype(jnp.bfloat16)
        dk = dot_tn(sg, q2)
        dv = dot_tn(low, g2)
        acc_ref[0, id0] += dk[:NBR]
        acc_ref[1, id0] += dv[:NBR]
        acc_ref[0, id1] += dk[NBR:]
        acc_ref[1, id1] += dv[NBR:]
        return 0

    lax.fori_loop(0, spans, span, 0, unroll=4)

    def store(i, _):
        for j in range(2):
            dkv_ref[j, i] = acc_ref[j, i].astype(jnp.bfloat16)
        return 0

    lax.fori_loop(0, blocks, store, 0)


def attend(ids, queries, grads, kv):
    rows, cols = queries.shape
    blocks = kv.shape[1] * kv.shape[2] // NBR
    vmem = pl.BlockSpec(memory_space=pltpu.VMEM)
    context, query_grad, dkv = pl.pallas_call(
        attend_kernel,
        out_shape=(
            jax.ShapeDtypeStruct((rows, cols), jnp.bfloat16),
            jax.ShapeDtypeStruct((rows, cols), jnp.bfloat16),
            jax.ShapeDtypeStruct((2, blocks, NBR, cols), jnp.bfloat16),
        ),
        in_specs=[pl.BlockSpec(memory_space=pltpu.SMEM), vmem, vmem, vmem],
        out_specs=(vmem, vmem, vmem),
        scratch_shapes=[pltpu.VMEM((2, blocks, NBR, cols), jnp.float32)],
        compiler_params=pltpu.CompilerParams(vmem_limit_bytes=40 * MIB),
        name="attend",
    )(ids, queries, grads, kv.reshape(2, blocks, NBR, cols))
    return context, query_grad, dkv.reshape(kv.shape)


class Place:
    def __init__(self):
        self.seq = lax.axis_index("seq")
        self.head = lax.axis_index("head")
        x, z = lax.div(self.seq, SIDE), lax.div(self.head, 2)
        y, self.core = self.seq - x * SIDE, self.head - z * 2
        self.xs = [x] + [lax.rem(x + i, SIDE) for i in range(1, SIDE)]
        self.ys = [y] + [lax.rem(y + i, SIDE) for i in range(1, SIDE)]
        self.zs = [z] + [lax.rem(z + i, RING) for i in range(1, RING)]
        self.pairs = [2 * z for z in self.zs]
        self.rows = [SIDE * x for x in self.xs]
        self.other = (self.seq, self.pairs[0] + 1 - self.core)

    def along(self, is_x, step):
        return (self.slot(is_x, step, 0), self.head)

    def ring(self, step):
        return (self.seq, self.pairs[step % RING] + self.core)

    def twin(self):
        return self.other

    def slot(self, first_is_x, first, second):
        if not first_is_x:
            first, second = second, first
        return self.rows[first % SIDE] + self.ys[second % SIDE]


def greet(devices):
    barrier = pltpu.get_barrier_semaphore()
    for device in devices:
        pl.semaphore_signal(barrier, inc=1, device_id=device, device_id_type=MESH)
    pl.semaphore_wait(barrier, len(devices))


class Sender:
    def __init__(self, sems):
        self.sems = sems

    def send(self, src, dst, group, recv_sem, device):
        pltpu.make_async_remote_copy(
            src_ref=src,
            dst_ref=dst,
            send_sem=self.sems.at[group],
            recv_sem=recv_sem,
            device_id=device,
            device_id_type=MESH,
        ).start()

    def finish(self, ref, group, recv_sem, device):
        pltpu.make_async_remote_copy(
            src_ref=ref,
            dst_ref=ref,
            send_sem=self.sems.at[group],
            recv_sem=recv_sem,
            device_id=device,
            device_id_type=MESH,
        ).wait_send()


def arrived(ref, send_sem, recv_sem, device):
    pltpu.make_async_remote_copy(
        src_ref=ref, dst_ref=ref, send_sem=send_sem, recv_sem=recv_sem, device_id=device, device_id_type=MESH
    ).wait_recv()


class Gather:
    def __init__(self, place, sender, group, buf, recv, j, first_is_x, row, rows, sign, together):
        self.place, self.sender, self.group, self.buf, self.recv = place, sender, group, buf, recv
        self.j, self.fx, self.row, self.rows, self.sign, self.together = j, first_is_x, row, rows, sign, together

    def ref(self, slot):
        return self.buf.at[self.j, slot, pl.ds(self.row, self.rows), :]

    def send(self, offsets, kind, is_x, step):
        slot = self.place.slot(self.fx, *offsets)
        self.sender.send(self.ref(slot), self.ref(slot), self.group, self.recv(kind), self.place.along(is_x, step))

    def wait(self, offsets, kind):
        ref = self.ref(self.place.slot(self.fx, *offsets))
        arrived(ref, self.sender.sems.at[0], self.recv(kind), self.place.twin())

    def relays(self):
        return [0, -self.sign, self.sign, 2]

    def last(self, i, second):
        return 7 if self.together else 7 + 2 * i + second - 1

    def spread(self, i):
        first = self.relays()[i]
        self.send((first, 0), 3 + i, not self.fx, self.sign)
        self.send((first, 0), self.last(i, 1), not self.fx, -self.sign)

    def begin(self):
        self.send((0, 0), 0, self.fx, self.sign)
        self.send((0, 0), 1, self.fx, -self.sign)
        self.spread(0)

    def near(self, which):
        if which == 1:
            self.wait((-self.sign, 0), 0)
            self.send((-self.sign, 0), 2, self.fx, self.sign)
        else:
            self.wait((self.sign, 0), 1)
        self.spread(which)

    def far(self):
        self.wait((-2 * self.sign, 0), 2)
        self.spread(3)

    def relay(self, i):
        first = self.relays()[i]
        self.wait((first, -self.sign), 3 + i)
        self.send((first, -self.sign), self.last(i, 2), not self.fx, self.sign)

    def rest(self, i, second):
        self.wait((self.relays()[i], self.sign * second), self.last(i, second))


class Ring:
    def __init__(self, place, sender, groups, at, ring_recv, twin_recv, rows):
        self.place, self.sender, self.groups, self.at = place, sender, groups, at
        self.ring_recv, self.twin_recv, self.rows = ring_recv, twin_recv, rows

    def slot(self, distance, other):
        core = 1 - self.place.core if other else self.place.core
        return self.place.pairs[distance % RING] + core

    def unit(self, slot, b, u):
        half = self.rows // 2
        return self.at(slot, b * self.rows + u * half, half)

    def batch(self, slot, b):
        return self.at(slot, b * self.rows, self.rows)

    def signs(self, d, u):
        return (1, -1) if d < RING // 2 else ((1,) if u == 0 else (-1,))

    def ring_sem(self, sign, d, b, u):
        return self.ring_recv.at[0 if sign > 0 else 1, d - 1, 2 * b + u]

    def to_ring(self, slot, d, b, u, sign):
        ref = self.unit(slot, b, u)
        self.sender.send(ref, ref, self.groups[0] + b, self.ring_sem(sign, d, b, u), self.place.ring(sign))

    def to_twin(self, distance, b):
        ref = self.batch(self.slot(distance, False), b)
        self.sender.send(ref, ref, self.groups[1] + b, self.twin_recv(distance, b), self.place.twin())

    def start(self, b):
        for u in range(2):
            for sign in (1, -1):
                self.to_ring(self.place.head, 1, b, u, sign)
        self.to_twin(0, b)

    def relay(self, b, d, u, sign):
        slot = self.slot(-sign * d, False)
        arrived(self.unit(slot, b, u), self.sender.sems.at[0], self.ring_sem(sign, d, b, u), self.place.twin())
        if d < RING // 2 and sign in self.signs(d + 1, u):
            self.to_ring(slot, d + 1, b, u, sign)

    def hop(self, b, d):
        for u in range(2):
            for sign in self.signs(d, u):
                self.relay(b, d, u, sign)
        for distance in (-d, d) if d < RING // 2 else (d,):
            self.to_twin(distance, b)

    def from_twin(self, b, distance):
        slot = self.slot(distance, True)
        arrived(self.batch(slot, b), self.sender.sems.at[0], self.twin_recv(distance, b), self.place.twin())


def pool_kernel(
    states_ref, kw_ref, vw_ref, kv_ref, part_ref, st, shares, mid, w, acc,
    send_sems, twin_recv, ring_recv, pool_recv, swap_recv, w_sems,
):
    place = Place()
    rows, feats = st.shape[1:]
    cols = kv_ref.shape[3]
    batches = BATCHES
    batch = rows // batches
    loads = [pltpu.make_async_copy(kw_ref, w.at[0], w_sems.at[0]), pltpu.make_async_copy(vw_ref, w.at[1], w_sems.at[1])]
    for load in loads:
        load.start()
    st[place.head] = states_ref[...]
    acc[...] = jnp.zeros_like(acc)
    greet(
        [place.ring(1), place.ring(-1), place.twin()]
        + [place.along(i, d) for i in (True, False) for d in (1, -1, 2)]
    )
    sender = Sender(send_sems)

    def at(slot, row, n):
        return st.at[slot, pl.ds(row, n), :]

    def twin_sem(distance, b):
        return twin_recv.at[distance + RING // 2 - 1, b]

    ring = Ring(place, sender, (0, batches), at, ring_recv, twin_sem, batch)

    def multiply(slot, b):
        here = pl.ds(b * batch, batch)
        left = st[slot, here, :]
        acc[here, :cols] += dot_nn(left, w[0, slot])
        acc[here, cols:] += dot_nn(left, w[1, slot])

    def own(b, distance):
        multiply(ring.slot(distance, False), b)

    def other(b, distance):
        ring.from_twin(b, distance)
        multiply(ring.slot(distance, True), b)

    def twin(b, distance):
        ring.to_twin(distance, b)

    def project(b):
        here = pl.ds(b * batch, batch)
        kv_ref[0, place.seq, here, :] = acc[here, :cols].astype(kv_ref.dtype)
        kv_ref[1, place.seq, here, :] = acc[here, cols:].astype(kv_ref.dtype)
        for one in gathers[b]:
            one.begin()

    def gather(b, j):
        sign = 1 if (b + j) % 2 == 0 else -1
        recv = lambda kind: pool_recv.at[b, j, kind]
        return Gather(place, sender, 2 * batches + b, kv_ref, recv, j, j == 0, b * batch, batch, sign, True)

    gathers = [[gather(b, j) for j in range(2)] for b in range(batches)]

    share = rows // (SIDE * SIDE)
    mine = pl.ds(pl.multiple_of(place.head * share, share), share)
    side = [pl.ds(0, feats // 2), pl.ds(feats // 2, feats // 2)]
    here = (place.xs, place.ys)
    steps = (2, 1, -1)

    def gather_share():
        for slot in range(SIDE * SIDE):
            x, y = slot // SIDE, slot % SIDE
            shares[0, x, y] = st[slot, mine, side[0]]
            shares[1, y, x] = st[slot, mine, side[1]]

    def column(j, source):
        return part_ref.at[:, source, :, side[j]] if j == 0 else part_ref.at[source, :, :, side[j]]

    def swap_first():
        gather_share()
        for i, step in enumerate(steps):
            for j in range(2):
                sender.send(
                    shares.at[j, here[j][step % SIDE]], mid.at[j, here[j][0]], 3 * batches,
                    swap_recv.at[j, 0, i], place.along(j == 0, step),
                )
        for j in range(2):
            mid[j, here[j][0]] = shares[j, here[j][0]]

    def swap_second():
        for i, step in enumerate(steps):
            for j in range(2):
                arrived(mid.at[j, here[j][-step % SIDE]], send_sems.at[0], swap_recv.at[j, 0, i], place.twin())
        for i, step in enumerate(steps):
            for j in range(2):
                sender.send(
                    mid.at[j, :, here[1 - j][step % SIDE]], column(j, here[1 - j][0]), 3 * batches,
                    swap_recv.at[j, 1, i], place.along(j != 0, step),
                )
        for j in range(2):
            column(j, here[1 - j][0])[...] = mid[j, :, here[1 - j][0]]

    def swap_end():
        for i, step in enumerate(steps):
            for j in range(2):
                arrived(column(j, here[1 - j][-step % SIDE]), send_sems.at[0], swap_recv.at[j, 1, i], place.twin())

    steps_of = {
        "start": ring.start,
        "hop": ring.relay,
        "twin": twin,
        "own": own,
        "other": other,
        "project": project,
        "near1": lambda b, j: gathers[b][j].near(1),
        "near2": lambda b, j: gathers[b][j].near(2),
        "far": lambda b, j: gathers[b][j].far(),
        "relay": lambda b, j, i: gathers[b][j].relay(i),
        "swap": lambda i: (swap_first, swap_second)[i](),
    }
    waiting = list(loads)
    for name, *what in ORDER:
        if name in ("own", "other") and waiting:
            for load in waiting:
                load.wait()
            waiting = []
        steps_of[name](*what)
    swap_end()
    for b in range(batches):
        for j in range(2):
            arrived(kv_ref.at[j, pl.ds(0, 8), pl.ds(0, batch), :], send_sems.at[0], pool_recv.at[b, j, 7], place.twin())
    spare = (swap_recv.at[0, 0, 0], place.twin())
    for b in range(batches):
        sender.finish(st.at[pl.ds(0, RING - 1), pl.ds(0, batch), :], b, *spare)
        sender.finish(st.at[pl.ds(0, RING), pl.ds(0, batch), :], batches + b, *spare)
        sender.finish(kv_ref.at[0, pl.ds(0, 15), pl.ds(0, 2 * batch), :], 2 * batches + b, *spare)
    sender.finish(st.at[pl.ds(0, 6), pl.ds(0, SIDE * share), :], 3 * batches, *spare)


def pool(states, key_weight, value_weight):
    rows, feats = states.shape
    cols = key_weight.shape[1]
    heads = key_weight.shape[0] // feats
    seqs = SIDE * SIDE
    share = rows // heads
    vmem, hbm = pl.BlockSpec(memory_space=pltpu.VMEM), pl.BlockSpec(memory_space=pltpu.HBM)
    dma = pltpu.SemaphoreType.DMA
    return pl.pallas_call(
        pool_kernel,
        out_shape=(
            jax.ShapeDtypeStruct((2, seqs, rows, cols), jnp.bfloat16),
            jax.ShapeDtypeStruct((SIDE, SIDE, share, feats), jnp.bfloat16),
        ),
        in_specs=[vmem, hbm, hbm],
        out_specs=(vmem, vmem),
        scratch_shapes=[
            pltpu.VMEM((heads, rows, feats), jnp.bfloat16),
            pltpu.VMEM((2, SIDE, SIDE, share, feats // 2), jnp.bfloat16),
            pltpu.VMEM((2, SIDE, SIDE, share, feats // 2), jnp.bfloat16),
            pltpu.VMEM((2, heads, feats, cols), jnp.bfloat16),
            pltpu.VMEM((rows, 2 * cols), jnp.float32),
            dma((3 * BATCHES + 1,)),
            dma((RING, BATCHES)),
            dma((2, RING // 2, 2 * BATCHES)),
            dma((BATCHES, 2, 8)),
            dma((2, 2, 3)),
            dma((2,)),
        ],
        compiler_params=pltpu.CompilerParams(
            collective_id=1, has_side_effects=True, vmem_limit_bytes=48 * MIB
        ),
        name="pool",
    )(states, key_weight.reshape(heads, feats, cols), value_weight.reshape(heads, feats, cols))


def reduce_kernel(
    dkv_ref, part_ref, dk_ref, dv_ref, pooled, t, box, mid, box2,
    send_sems, box_recv, box2_recv, pool_recv, twin_recv, ring_recv,
):
    place = Place()
    rows, cols = dkv_ref.shape[2], dkv_ref.shape[3]
    heads, feats = t.shape[0], t.shape[2]
    share = rows // heads
    half = rows // 2
    halves = (pl.ds(0, half), pl.ds(half, half))
    offsets = (2, 1, 3, 0)
    t[place.head] = part_ref[...]
    greet(
        [place.along(i, d) for i in (True, False) for d in (1, -1)] + [place.ring(1), place.ring(-1), place.twin()]
    )
    sender = Sender(send_sems)
    ways = ((0, 1), (1, -1))
    ring = Ring(
        place, sender, (4, 5), lambda slot, row, n: t.at[slot, pl.ds(row, n), :], ring_recv,
        lambda distance, b: twin_recv.at[0], rows,
    )

    def add(*terms):
        total = terms[0].astype(jnp.float32)
        for term in terms[1:]:
            total = total + term.astype(jnp.float32)
        return total.astype(jnp.bfloat16)

    def send1(j, way, sign, kind, k, src):
        sender.send(src, box.at[j, way, kind, k], 0, box_recv.at[j, way, kind, k], place.along(j == 0, sign))

    def wait1(j, way, kind, k):
        arrived(box.at[j, way, kind, k], send_sems.at[0], box_recv.at[j, way, kind, k], place.along(j == 0, 1))

    def send2(j, way, sign, kind, src):
        sender.send(src, box2.at[j, way, kind], 1, box2_recv.at[j, way, kind], place.along(j != 0, sign))

    def wait2(j, way, kind):
        arrived(box2.at[j, way, kind], send_sems.at[0], box2_recv.at[j, way, kind], place.along(j != 0, 1))

    for k, second in enumerate(offsets):
        for j in range(2):
            for way, sign in ways:
                send1(j, way, sign, 0, k, dkv_ref.at[j, place.slot(j == 0, 2, second), halves[way], :])
    for k, second in enumerate(offsets):
        for j in range(2):
            for way, sign in ways:
                send1(j, way, sign, 1, k, dkv_ref.at[j, place.slot(j == 0, sign, second), halves[1 - way], :])
    ring.start(0)
    for k, second in enumerate(offsets):
        for j in range(2):
            for way, sign in ways:
                wait1(j, way, 0, k)
                mine = dkv_ref[j, place.slot(j == 0, sign, second), halves[way], :]
                box[j, way, 0, k] = add(box[j, way, 0, k], mine)
                send1(j, way, sign, 2, k, box.at[j, way, 0, k])
    dk_ref[...] = jnp.zeros_like(dk_ref)
    dv_ref[...] = jnp.zeros_like(dv_ref)
    ring.hop(0, 1)
    for k, second in enumerate(offsets):
        for j in range(2):
            for way, sign in ways:
                wait1(j, 1 - way, 1, k)
                wait1(j, way, 2, k)
                mine = dkv_ref[j, place.slot(j == 0, 0, second), halves[way], :]
                mid[j, k, halves[way], :] = add(mine, box[j, 1 - way, 1, k], box[j, way, 2, k])
            if k == 0:
                for way, sign in ways:
                    send2(j, way, sign, 0, mid.at[j, 0, halves[way], :])
            if k in (1, 2):
                way, sign = ways[k - 1]
                send2(j, way, sign, 1, mid.at[j, k, halves[1 - way], :])
        if k == 1:
            ring.hop(0, 2)
    for j in range(2):
        for way, sign in ways:
            wait2(j, way, 0)
            box2[j, way, 0] = add(box2[j, way, 0], mid[j, 1 + way, halves[way], :])
            send2(j, way, sign, 2, box2.at[j, way, 0])
    ring.hop(0, 3)

    def gather(way, sign, j):
        recv = lambda kind: pool_recv.at[way, j, kind]
        return Gather(place, sender, 2 + j, pooled, recv, j, j != 0, way * half, half, sign, False)

    gathers = []
    for way, sign in ways:
        for j in range(2):
            wait2(j, 1 - way, 1)
            wait2(j, way, 2)
            pooled[j, place.seq, halves[way], :] = add(
                mid[j, 3, halves[way], :], box2[j, 1 - way, 1], box2[j, way, 2]
            )
            gathers.append(gather(way, sign, j))
            gathers[-1].begin()

    def near():
        for which in (1, 2):
            for one in gathers:
                one.near(which)

    def far():
        for one in gathers:
            one.far()

    def relay(i):
        for one in gathers:
            one.relay(i)

    def rest(i, second):
        for one in gathers:
            one.rest(i, second)

    def multiply(x, y):
        slot = place.slot(True, x, y)
        left = t[:, pl.ds(pl.multiple_of(slot * share, share), share), :].reshape(rows, feats)
        right = jnp.concatenate([pooled[0, slot], pooled[1, slot]], axis=1)
        product = dot_tn(left, right)
        dk_ref[...] += product[:, :cols]
        dv_ref[...] += product[:, cols:]

    near()
    ring.hop(0, 4)
    relay(0)
    arrived(t.at[pl.ds(0, RING)], send_sems.at[0], twin_recv.at[0], place.twin())
    multiply(0, 0)
    far()
    relay(1)
    relay(2)
    rest(0, 1)
    for step in (1, -1):
        multiply(step, 0)
        multiply(0, step)
    relay(3)
    rest(0, 2)
    multiply(2, 0)
    multiply(0, 2)
    rest(1, 1)
    rest(2, 1)
    for x in (1, -1):
        for y in (1, -1):
            multiply(x, y)
    rest(1, 2)
    rest(2, 2)
    rest(3, 1)
    for step in (1, -1):
        multiply(step, 2)
        multiply(2, step)
    rest(3, 2)
    multiply(2, 2)
    spare = (twin_recv.at[0], place.twin())
    sender.finish(box, 0, *spare)
    sender.finish(box2, 1, *spare)
    for j in range(2):
        sender.finish(pooled.at[j, pl.ds(0, 15)], 2 + j, *spare)
    sender.finish(t.at[pl.ds(0, RING - 1)], 4, *spare)
    sender.finish(t.at[pl.ds(0, RING)], 5, *spare)


def weight_grads(dkv, part):
    _, seqs, rows, cols = dkv.shape
    feats = part.shape[1]
    heads = 2 * RING
    half = rows // 2
    vmem = pl.BlockSpec(memory_space=pltpu.VMEM)
    dma = pltpu.SemaphoreType.DMA
    return pl.pallas_call(
        reduce_kernel,
        out_shape=(jax.ShapeDtypeStruct((feats, cols), jnp.float32),) * 2,
        in_specs=[vmem, vmem],
        out_specs=(vmem, vmem),
        scratch_shapes=[
            pltpu.VMEM((2, seqs, rows, cols), jnp.bfloat16),
            pltpu.VMEM((heads, rows, feats), jnp.bfloat16),
            pltpu.VMEM((2, 2, 3, SIDE, half, cols), jnp.bfloat16),
            pltpu.VMEM((2, SIDE, rows, cols), jnp.bfloat16),
            pltpu.VMEM((2, 2, 3, half, cols), jnp.bfloat16),
            dma((6,)),
            dma((2, 2, 3, SIDE)),
            dma((2, 2, 3)),
            dma((2, 2, 15)),
            dma((1,)),
            dma((2, RING // 2, 2)),
        ],
        compiler_params=pltpu.CompilerParams(
            collective_id=2, has_side_effects=True, vmem_limit_bytes=32 * MIB
        ),
        name="reduce_all",
    )(dkv, part)


def local(queries, states, key_weight, value_weight, neighbour_ids, out_grad):
    kv, part = pool(states, key_weight, value_weight)
    context, query_grad, dkv = attend(neighbour_ids.T, queries, out_grad, kv)
    dk, dv = weight_grads(dkv, part.reshape(states.shape))
    return context, query_grad, dk, dv


def solution(mesh):
    in_specs = (
        P("seq", "head"),
        P("seq", "head"),
        P(None, "head"),
        P(None, "head"),
        P("seq", None),
        P("seq", "head"),
    )
    out_specs = (P("seq", "head"), P("seq", "head"), P("seq", "head"), P("seq", "head"))
    return jax.shard_map(local, mesh=mesh, in_specs=in_specs, out_specs=out_specs, check_vma=False)
```

```python
import math

import jax
import jax.numpy as jnp
from jax import lax
from jax.experimental import pallas as pl
from jax.experimental.pallas import tpu as pltpu
from jax.sharding import PartitionSpec as P

HD = 128
SPAN = 64
NBR = 128
TOPN = 2
SCALE = 1.0 / math.sqrt(HD)
MIB = 1 << 20
MESH = pl.DeviceIdType.MESH
SIDE = 4
RING = 8
BATCHES = 4
ORDER = (
    ("start", 0), ("start", 1), ("hop", 0, 1, 0, 1), ("hop", 0, 1, 0, -1), ("hop", 0, 1, 1, 1), ("hop", 0, 1, 1, -1),
    ("twin", 0, -1), ("twin", 0, 1), ("hop", 1, 1, 0, 1), ("hop", 1, 1, 0, -1), ("hop", 1, 1, 1, 1),
    ("hop", 1, 1, 1, -1), ("twin", 1, -1), ("twin", 1, 1), ("other", 0, -1), ("other", 0, 0), ("own", 0, -1),
    ("hop", 0, 2, 0, 1), ("hop", 0, 2, 0, -1), ("own", 0, 0), ("own", 0, 1), ("other", 0, 1), ("hop", 0, 2, 1, 1),
    ("hop", 0, 2, 1, -1), ("twin", 0, -2), ("twin", 0, 2), ("own", 0, -2), ("own", 0, 2), ("other", 1, 0),
    ("hop", 1, 2, 0, 1), ("hop", 1, 2, 0, -1), ("own", 1, -1), ("own", 1, 0), ("own", 1, 1), ("hop", 1, 2, 1, 1),
    ("hop", 1, 2, 1, -1), ("twin", 1, -2), ("twin", 1, 2), ("other", 0, -2), ("other", 0, 2), ("hop", 0, 3, 0, 1),
    ("hop", 0, 3, 0, -1), ("own", 1, -2), ("own", 1, 2), ("other", 1, -1), ("hop", 0, 3, 1, 1), ("hop", 0, 3, 1, -1),
    ("twin", 0, -3), ("twin", 0, 3), ("own", 0, -3), ("own", 0, 3), ("other", 1, 1), ("hop", 1, 3, 0, 1),
    ("hop", 1, 3, 0, -1), ("other", 1, -2), ("other", 1, 2), ("own", 2, 0), ("hop", 1, 3, 1, 1), ("twin", 1, -3),
    ("hop", 1, 3, 1, -1), ("twin", 1, 3), ("other", 0, -3), ("start", 2), ("other", 0, 3), ("hop", 0, 4, 0, 1),
    ("own", 1, -3), ("own", 1, 3), ("own", 3, 0), ("hop", 0, 4, 1, -1), ("twin", 0, 4), ("own", 0, 4),
    ("other", 1, -3), ("start", 3), ("hop", 1, 4, 0, 1), ("other", 1, 3), ("other", 2, 0), ("hop", 1, 4, 1, -1),
    ("twin", 1, 4), ("other", 0, 4), ("project", 0), ("hop", 2, 1, 0, 1), ("hop", 2, 1, 0, -1), ("own", 1, 4),
    ("hop", 2, 1, 1, 1), ("twin", 2, -1), ("own", 2, -1), ("other", 3, 0), ("hop", 2, 1, 1, -1), ("twin", 2, 1),
    ("other", 1, 4), ("hop", 3, 1, 0, 1), ("project", 1), ("hop", 3, 1, 0, -1), ("hop", 3, 1, 1, 1), ("twin", 3, -1),
    ("own", 2, 1), ("other", 2, -1), ("hop", 3, 1, 1, -1), ("twin", 3, 1), ("near1", 0, 0), ("near2", 0, 0),
    ("relay", 0, 0, 0), ("hop", 2, 2, 0, 1), ("other", 2, 1), ("hop", 2, 2, 0, -1), ("relay", 0, 1, 0),
    ("near2", 0, 1), ("near1", 0, 1), ("hop", 2, 2, 1, 1), ("twin", 2, -2), ("hop", 2, 2, 1, -1), ("twin", 2, 2),
    ("own", 2, -2), ("own", 2, 2), ("near1", 1, 0), ("hop", 3, 2, 0, 1), ("near2", 1, 0), ("hop", 3, 2, 0, -1),
    ("relay", 1, 0, 0), ("own", 3, -1), ("own", 3, 1), ("hop", 3, 2, 1, 1), ("twin", 3, -2), ("relay", 1, 1, 0),
    ("hop", 3, 2, 1, -1), ("twin", 3, 2), ("near2", 1, 1), ("near1", 1, 1), ("far", 0, 0), ("hop", 2, 3, 0, 1),
    ("relay", 0, 0, 1), ("other", 2, -2), ("hop", 2, 3, 0, -1), ("other", 2, 2), ("own", 3, -2), ("hop", 2, 3, 1, 1),
    ("twin", 2, -3), ("relay", 0, 0, 2), ("hop", 2, 3, 1, -1), ("twin", 2, 3), ("relay", 0, 1, 2), ("own", 2, -3),
    ("own", 2, 3), ("hop", 3, 3, 0, 1), ("far", 0, 1), ("hop", 3, 3, 0, -1), ("relay", 0, 1, 1), ("own", 3, 2),
    ("other", 3, -1), ("hop", 3, 3, 1, 1), ("twin", 3, -3), ("relay", 1, 0, 1), ("other", 2, -3),
    ("hop", 3, 3, 1, -1), ("twin", 3, 3), ("far", 1, 0), ("relay", 1, 0, 2), ("hop", 2, 4, 0, 1), ("relay", 1, 1, 2),
    ("other", 2, 3), ("own", 3, -3), ("own", 3, 3), ("other", 3, 1), ("hop", 2, 4, 1, -1), ("twin", 2, 4),
    ("far", 1, 1), ("relay", 1, 1, 1), ("own", 2, 4), ("other", 3, -2), ("hop", 3, 4, 0, 1), ("relay", 0, 0, 3),
    ("other", 3, 2), ("other", 3, -3), ("other", 3, 3), ("other", 2, 4), ("hop", 3, 4, 1, -1), ("twin", 3, 4),
    ("project", 2), ("relay", 0, 1, 3), ("relay", 1, 0, 3), ("own", 3, 4), ("relay", 1, 1, 3), ("other", 3, 4),
    ("project", 3), ("swap", 0), ("near1", 2, 0), ("near2", 2, 0), ("relay", 2, 0, 0), ("relay", 2, 1, 0),
    ("near2", 2, 1), ("near1", 2, 1), ("near2", 3, 0), ("near1", 3, 0), ("relay", 3, 0, 0), ("near1", 3, 1),
    ("relay", 3, 1, 0), ("near2", 3, 1), ("swap", 1), ("relay", 2, 0, 1), ("far", 2, 0), ("relay", 2, 0, 2),
    ("relay", 2, 1, 2), ("relay", 2, 1, 1), ("far", 2, 1), ("relay", 3, 1, 1), ("far", 3, 0), ("relay", 3, 0, 2),
    ("relay", 3, 0, 1), ("far", 3, 1), ("relay", 3, 1, 2), ("relay", 2, 0, 3), ("relay", 3, 0, 3), ("relay", 2, 1, 3),
    ("relay", 3, 1, 3),
)


def dot_nt(a, b):
    return lax.dot_general(a, b, (((1,), (1,)), ((), ())), preferred_element_type=jnp.float32)


def dot_tn(a, b):
    return lax.dot_general(a, b, (((0,), (0,)), ((), ())), preferred_element_type=jnp.float32)


def dot_nn(a, b):
    return jnp.dot(a, b, preferred_element_type=jnp.float32)


def attend_kernel(ids_ref, q_ref, g_ref, kv_ref, ctx_ref, dq_ref, dkv_ref, acc_ref):
    cols = q_ref.shape[1]
    spans = q_ref.shape[0] // SPAN
    blocks = kv_ref.shape[1]
    first = lax.broadcasted_iota(jnp.int32, (SPAN, cols), 1) < HD

    def clear(i, _):
        for j in range(2):
            acc_ref[j, i] = jnp.zeros((NBR, cols), jnp.float32)
        return 0

    lax.fori_loop(0, blocks, clear, 0)

    def stack(x):
        zero = jnp.zeros_like(x)
        return jnp.concatenate([jnp.where(first, x, zero), jnp.where(first, zero, x)], axis=0)

    def unstack(x):
        return jnp.where(first, x[:SPAN], x[SPAN:])

    def span(c, _):
        rows = pl.ds(c * SPAN, SPAN)
        id0, id1 = ids_ref[0, c], ids_ref[1, c]
        keys = jnp.concatenate([kv_ref[0, id0], kv_ref[0, id1]], axis=0)
        values = jnp.concatenate([kv_ref[1, id0], kv_ref[1, id1]], axis=0)
        q2 = stack(q_ref[rows, :])
        g2 = stack(g_ref[rows, :])
        scores = dot_nt(q2, keys) * SCALE
        prob_grad = dot_nt(g2, values)
        top = jnp.max(scores, axis=-1, keepdims=True)
        e = jnp.exp(scores - top)
        probs = e * (1.0 / jnp.sum(e, axis=-1, keepdims=True))
        low = probs.astype(jnp.bfloat16)
        delta = jnp.sum(probs * prob_grad, axis=-1, keepdims=True)
        sg = (probs * (prob_grad - delta) * SCALE).astype(jnp.bfloat16)
        ctx_ref[rows, :] = unstack(dot_nn(low, values)).astype(jnp.bfloat16)
        dq_ref[rows, :] = unstack(dot_nn(sg, keys)).astype(jnp.bfloat16)
        dk = dot_tn(sg, q2)
        dv = dot_tn(low, g2)
        acc_ref[0, id0] += dk[:NBR]
        acc_ref[1, id0] += dv[:NBR]
        acc_ref[0, id1] += dk[NBR:]
        acc_ref[1, id1] += dv[NBR:]
        return 0

    lax.fori_loop(0, spans, span, 0, unroll=8)

    def store(i, _):
        for j in range(2):
            dkv_ref[j, i] = acc_ref[j, i].astype(jnp.bfloat16)
        return 0

    lax.fori_loop(0, blocks, store, 0)


def attend(ids, queries, grads, kv):
    rows, cols = queries.shape
    blocks = kv.shape[1] * kv.shape[2] // NBR
    vmem = pl.BlockSpec(memory_space=pltpu.VMEM)
    context, query_grad, dkv = pl.pallas_call(
        attend_kernel,
        out_shape=(
            jax.ShapeDtypeStruct((rows, cols), jnp.bfloat16),
            jax.ShapeDtypeStruct((rows, cols), jnp.bfloat16),
            jax.ShapeDtypeStruct((2, blocks, NBR, cols), jnp.bfloat16),
        ),
        in_specs=[pl.BlockSpec(memory_space=pltpu.SMEM), vmem, vmem, vmem],
        out_specs=(vmem, vmem, vmem),
        scratch_shapes=[pltpu.VMEM((2, blocks, NBR, cols), jnp.float32)],
        compiler_params=pltpu.CompilerParams(vmem_limit_bytes=40 * MIB),
        name="attend",
    )(ids, queries, grads, kv.reshape(2, blocks, NBR, cols))
    return context, query_grad, dkv.reshape(kv.shape)


class Place:
    def __init__(self):
        self.seq = lax.axis_index("seq")
        self.head = lax.axis_index("head")
        x, z = lax.div(self.seq, SIDE), lax.div(self.head, 2)
        y, self.core = self.seq - x * SIDE, self.head - z * 2
        self.xs = [x] + [lax.rem(x + i, SIDE) for i in range(1, SIDE)]
        self.ys = [y] + [lax.rem(y + i, SIDE) for i in range(1, SIDE)]
        self.zs = [z] + [lax.rem(z + i, RING) for i in range(1, RING)]
        self.pairs = [2 * z for z in self.zs]
        self.rows = [SIDE * x for x in self.xs]
        self.other = (self.seq, self.pairs[0] + 1 - self.core)

    def along(self, is_x, step):
        return (self.slot(is_x, step, 0), self.head)

    def ring(self, step):
        return (self.seq, self.pairs[step % RING] + self.core)

    def twin(self):
        return self.other

    def slot(self, first_is_x, first, second):
        if not first_is_x:
            first, second = second, first
        return self.rows[first % SIDE] + self.ys[second % SIDE]


def greet(devices):
    barrier = pltpu.get_barrier_semaphore()
    for device in devices:
        pl.semaphore_signal(barrier, inc=1, device_id=device, device_id_type=MESH)
    pl.semaphore_wait(barrier, len(devices))


class Sender:
    def __init__(self, sems):
        self.sems = sems

    def send(self, src, dst, group, recv_sem, device):
        pltpu.make_async_remote_copy(
            src_ref=src,
            dst_ref=dst,
            send_sem=self.sems.at[group],
            recv_sem=recv_sem,
            device_id=device,
            device_id_type=MESH,
        ).start()

    def finish(self, ref, group, recv_sem, device):
        pltpu.make_async_remote_copy(
            src_ref=ref,
            dst_ref=ref,
            send_sem=self.sems.at[group],
            recv_sem=recv_sem,
            device_id=device,
            device_id_type=MESH,
        ).wait_send()


def arrived(ref, send_sem, recv_sem, device):
    pltpu.make_async_remote_copy(
        src_ref=ref, dst_ref=ref, send_sem=send_sem, recv_sem=recv_sem, device_id=device, device_id_type=MESH
    ).wait_recv()


class Gather:
    def __init__(self, place, sender, group, buf, recv, j, first_is_x, row, rows, sign, together):
        self.place, self.sender, self.group, self.buf, self.recv = place, sender, group, buf, recv
        self.j, self.fx, self.row, self.rows, self.sign, self.together = j, first_is_x, row, rows, sign, together

    def ref(self, slot):
        return self.buf.at[self.j, slot, pl.ds(self.row, self.rows), :]

    def send(self, offsets, kind, is_x, step):
        slot = self.place.slot(self.fx, *offsets)
        self.sender.send(self.ref(slot), self.ref(slot), self.group, self.recv(kind), self.place.along(is_x, step))

    def wait(self, offsets, kind):
        ref = self.ref(self.place.slot(self.fx, *offsets))
        arrived(ref, self.sender.sems.at[0], self.recv(kind), self.place.twin())

    def relays(self):
        return [0, -self.sign, self.sign, 2]

    def last(self, i, second):
        return 7 if self.together else 7 + 2 * i + second - 1

    def spread(self, i):
        first = self.relays()[i]
        self.send((first, 0), 3 + i, not self.fx, self.sign)
        self.send((first, 0), self.last(i, 1), not self.fx, -self.sign)

    def begin(self):
        self.send((0, 0), 0, self.fx, self.sign)
        self.send((0, 0), 1, self.fx, -self.sign)
        self.spread(0)

    def near(self, which):
        if which == 1:
            self.wait((-self.sign, 0), 0)
            self.send((-self.sign, 0), 2, self.fx, self.sign)
        else:
            self.wait((self.sign, 0), 1)
        self.spread(which)

    def far(self):
        self.wait((-2 * self.sign, 0), 2)
        self.spread(3)

    def relay(self, i):
        first = self.relays()[i]
        self.wait((first, -self.sign), 3 + i)
        self.send((first, -self.sign), self.last(i, 2), not self.fx, self.sign)

    def rest(self, i, second):
        self.wait((self.relays()[i], self.sign * second), self.last(i, second))


class Ring:
    def __init__(self, place, sender, groups, at, ring_recv, twin_recv, rows):
        self.place, self.sender, self.groups, self.at = place, sender, groups, at
        self.ring_recv, self.twin_recv, self.rows = ring_recv, twin_recv, rows

    def slot(self, distance, other):
        core = 1 - self.place.core if other else self.place.core
        return self.place.pairs[distance % RING] + core

    def unit(self, slot, b, u):
        half = self.rows // 2
        return self.at(slot, b * self.rows + u * half, half)

    def batch(self, slot, b):
        return self.at(slot, b * self.rows, self.rows)

    def signs(self, d, u):
        return (1, -1) if d < RING // 2 else ((1,) if u == 0 else (-1,))

    def ring_sem(self, sign, d, b, u):
        return self.ring_recv.at[0 if sign > 0 else 1, d - 1, 2 * b + u]

    def to_ring(self, slot, d, b, u, sign):
        ref = self.unit(slot, b, u)
        self.sender.send(ref, ref, self.groups[0] + b, self.ring_sem(sign, d, b, u), self.place.ring(sign))

    def to_twin(self, distance, b):
        ref = self.batch(self.slot(distance, False), b)
        self.sender.send(ref, ref, self.groups[1] + b, self.twin_recv(distance, b), self.place.twin())

    def start(self, b):
        for u in range(2):
            for sign in (1, -1):
                self.to_ring(self.place.head, 1, b, u, sign)
        self.to_twin(0, b)

    def relay(self, b, d, u, sign):
        slot = self.slot(-sign * d, False)
        arrived(self.unit(slot, b, u), self.sender.sems.at[0], self.ring_sem(sign, d, b, u), self.place.twin())
        if d < RING // 2 and sign in self.signs(d + 1, u):
            self.to_ring(slot, d + 1, b, u, sign)

    def hop(self, b, d):
        for u in range(2):
            for sign in self.signs(d, u):
                self.relay(b, d, u, sign)
        for distance in (-d, d) if d < RING // 2 else (d,):
            self.to_twin(distance, b)

    def from_twin(self, b, distance):
        slot = self.slot(distance, True)
        arrived(self.batch(slot, b), self.sender.sems.at[0], self.twin_recv(distance, b), self.place.twin())


def pool_kernel(
    states_ref, kw_ref, vw_ref, kv_ref, part_ref, st, shares, mid, w, acc,
    send_sems, twin_recv, ring_recv, pool_recv, swap_recv, w_sems,
):
    place = Place()
    rows, feats = st.shape[1:]
    cols = kv_ref.shape[3]
    batches = BATCHES
    batch = rows // batches
    loads = [pltpu.make_async_copy(kw_ref, w.at[0], w_sems.at[0]), pltpu.make_async_copy(vw_ref, w.at[1], w_sems.at[1])]
    own_states = pltpu.make_async_copy(states_ref, st.at[place.head], w_sems.at[2])
    own_states.start()
    for load in loads:
        load.start()
    acc[...] = jnp.zeros_like(acc)
    greet(
        [place.ring(1), place.ring(-1), place.twin()]
        + [place.along(i, d) for i in (True, False) for d in (1, -1, 2)]
    )
    sender = Sender(send_sems)

    def at(slot, row, n):
        return st.at[slot, pl.ds(row, n), :]

    def twin_sem(distance, b):
        return twin_recv.at[distance + RING // 2 - 1, b]

    ring = Ring(place, sender, (0, batches), at, ring_recv, twin_sem, batch)

    def multiply(slot, b):
        here = pl.ds(b * batch, batch)
        left = st[slot, here, :]
        acc[here, :cols] += dot_nn(left, w[0, slot])
        acc[here, cols:] += dot_nn(left, w[1, slot])

    def own(b, distance):
        multiply(ring.slot(distance, False), b)

    def other(b, distance):
        ring.from_twin(b, distance)
        multiply(ring.slot(distance, True), b)

    def twin(b, distance):
        ring.to_twin(distance, b)

    def project(b):
        here = pl.ds(b * batch, batch)
        kv_ref[0, place.seq, here, :] = acc[here, :cols].astype(kv_ref.dtype)
        kv_ref[1, place.seq, here, :] = acc[here, cols:].astype(kv_ref.dtype)
        for one in gathers[b]:
            one.begin()

    def gather(b, j):
        sign = 1 if (b + j) % 2 == 0 else -1
        recv = lambda kind: pool_recv.at[b, j, kind]
        return Gather(place, sender, 2 * batches + b, kv_ref, recv, j, j == 0, b * batch, batch, sign, True)

    gathers = [[gather(b, j) for j in range(2)] for b in range(batches)]

    share = rows // (SIDE * SIDE)
    mine = pl.ds(pl.multiple_of(place.head * share, share), share)
    side = [pl.ds(0, feats // 2), pl.ds(feats // 2, feats // 2)]
    here = (place.xs, place.ys)
    steps = (2, 1, -1)

    def gather_share():
        for slot in range(SIDE * SIDE):
            x, y = slot // SIDE, slot % SIDE
            shares[0, x, y] = st[slot, mine, side[0]]
            shares[1, y, x] = st[slot, mine, side[1]]

    def column(j, source):
        return part_ref.at[:, source, :, side[j]] if j == 0 else part_ref.at[source, :, :, side[j]]

    def swap_first():
        gather_share()
        for i, step in enumerate(steps):
            for j in range(2):
                sender.send(
                    shares.at[j, here[j][step % SIDE]], mid.at[j, here[j][0]], 3 * batches,
                    swap_recv.at[j, 0, i], place.along(j == 0, step),
                )
        for j in range(2):
            mid[j, here[j][0]] = shares[j, here[j][0]]

    def swap_second():
        for i, step in enumerate(steps):
            for j in range(2):
                arrived(mid.at[j, here[j][-step % SIDE]], send_sems.at[0], swap_recv.at[j, 0, i], place.twin())
        for i, step in enumerate(steps):
            for j in range(2):
                sender.send(
                    mid.at[j, :, here[1 - j][step % SIDE]], column(j, here[1 - j][0]), 3 * batches,
                    swap_recv.at[j, 1, i], place.along(j != 0, step),
                )
        for j in range(2):
            column(j, here[1 - j][0])[...] = mid[j, :, here[1 - j][0]]

    def swap_end():
        for i, step in enumerate(steps):
            for j in range(2):
                arrived(column(j, here[1 - j][-step % SIDE]), send_sems.at[0], swap_recv.at[j, 1, i], place.twin())

    steps_of = {
        "start": ring.start,
        "hop": ring.relay,
        "twin": twin,
        "own": own,
        "other": other,
        "project": project,
        "near1": lambda b, j: gathers[b][j].near(1),
        "near2": lambda b, j: gathers[b][j].near(2),
        "far": lambda b, j: gathers[b][j].far(),
        "relay": lambda b, j, i: gathers[b][j].relay(i),
        "swap": lambda i: (swap_first, swap_second)[i](),
    }
    own_states.wait()
    waiting = list(loads)
    for name, *what in ORDER:
        if name in ("own", "other") and waiting:
            for load in waiting:
                load.wait()
            waiting = []
        steps_of[name](*what)
    swap_end()
    for b in range(batches):
        for j in range(2):
            arrived(kv_ref.at[j, pl.ds(0, 8), pl.ds(0, batch), :], send_sems.at[0], pool_recv.at[b, j, 7], place.twin())
    spare = (swap_recv.at[0, 0, 0], place.twin())
    for b in range(batches):
        sender.finish(st.at[pl.ds(0, RING - 1), pl.ds(0, batch), :], b, *spare)
        sender.finish(st.at[pl.ds(0, RING), pl.ds(0, batch), :], batches + b, *spare)
        sender.finish(kv_ref.at[0, pl.ds(0, 15), pl.ds(0, 2 * batch), :], 2 * batches + b, *spare)
    sender.finish(st.at[pl.ds(0, 6), pl.ds(0, SIDE * share), :], 3 * batches, *spare)


def pool(states, key_weight, value_weight):
    rows, feats = states.shape
    cols = key_weight.shape[1]
    heads = key_weight.shape[0] // feats
    seqs = SIDE * SIDE
    share = rows // heads
    vmem, hbm = pl.BlockSpec(memory_space=pltpu.VMEM), pl.BlockSpec(memory_space=pltpu.HBM)
    dma = pltpu.SemaphoreType.DMA
    return pl.pallas_call(
        pool_kernel,
        out_shape=(
            jax.ShapeDtypeStruct((2, seqs, rows, cols), jnp.bfloat16),
            jax.ShapeDtypeStruct((SIDE, SIDE, share, feats), jnp.bfloat16),
        ),
        in_specs=[hbm, hbm, hbm],
        out_specs=(vmem, vmem),
        scratch_shapes=[
            pltpu.VMEM((heads, rows, feats), jnp.bfloat16),
            pltpu.VMEM((2, SIDE, SIDE, share, feats // 2), jnp.bfloat16),
            pltpu.VMEM((2, SIDE, SIDE, share, feats // 2), jnp.bfloat16),
            pltpu.VMEM((2, heads, feats, cols), jnp.bfloat16),
            pltpu.VMEM((rows, 2 * cols), jnp.float32),
            dma((3 * BATCHES + 1,)),
            dma((RING, BATCHES)),
            dma((2, RING // 2, 2 * BATCHES)),
            dma((BATCHES, 2, 8)),
            dma((2, 2, 3)),
            dma((3,)),
        ],
        compiler_params=pltpu.CompilerParams(
            collective_id=1, has_side_effects=True, vmem_limit_bytes=48 * MIB
        ),
        name="pool",
    )(states, key_weight.reshape(heads, feats, cols), value_weight.reshape(heads, feats, cols))


def reduce_kernel(
    dkv_ref, part_ref, dk_ref, dv_ref, pooled, t, box, mid, box2,
    send_sems, box_recv, box2_recv, pool_recv, twin_recv, ring_recv,
):
    place = Place()
    rows, cols = dkv_ref.shape[2], dkv_ref.shape[3]
    heads, feats = t.shape[0], t.shape[2]
    share = rows // heads
    half = rows // 2
    halves = (pl.ds(0, half), pl.ds(half, half))
    offsets = (2, 1, 3, 0)
    t[place.head] = part_ref[...]
    greet(
        [place.along(i, d) for i in (True, False) for d in (1, -1)] + [place.ring(1), place.ring(-1), place.twin()]
    )
    sender = Sender(send_sems)
    ways = ((0, 1), (1, -1))
    ring = Ring(
        place, sender, (4, 5), lambda slot, row, n: t.at[slot, pl.ds(row, n), :], ring_recv,
        lambda distance, b: twin_recv.at[0], rows,
    )

    def add(*terms):
        total = terms[0].astype(jnp.float32)
        for term in terms[1:]:
            total = total + term.astype(jnp.float32)
        return total.astype(jnp.bfloat16)

    def send1(j, way, sign, kind, k, src):
        sender.send(src, box.at[j, way, kind, k], 0, box_recv.at[j, way, kind, k], place.along(j == 0, sign))

    def wait1(j, way, kind, k):
        arrived(box.at[j, way, kind, k], send_sems.at[0], box_recv.at[j, way, kind, k], place.along(j == 0, 1))

    def send2(j, way, sign, kind, src):
        sender.send(src, box2.at[j, way, kind], 1, box2_recv.at[j, way, kind], place.along(j != 0, sign))

    def wait2(j, way, kind):
        arrived(box2.at[j, way, kind], send_sems.at[0], box2_recv.at[j, way, kind], place.along(j != 0, 1))

    for k, second in enumerate(offsets):
        for j in range(2):
            for way, sign in ways:
                send1(j, way, sign, 0, k, dkv_ref.at[j, place.slot(j == 0, 2, second), halves[way], :])
    for k, second in enumerate(offsets):
        for j in range(2):
            for way, sign in ways:
                send1(j, way, sign, 1, k, dkv_ref.at[j, place.slot(j == 0, sign, second), halves[1 - way], :])
    ring.start(0)
    for k, second in enumerate(offsets):
        for j in range(2):
            for way, sign in ways:
                wait1(j, way, 0, k)
                mine = dkv_ref[j, place.slot(j == 0, sign, second), halves[way], :]
                box[j, way, 0, k] = add(box[j, way, 0, k], mine)
                send1(j, way, sign, 2, k, box.at[j, way, 0, k])
    dk_ref[...] = jnp.zeros_like(dk_ref)
    dv_ref[...] = jnp.zeros_like(dv_ref)
    ring.hop(0, 1)
    for k, second in enumerate(offsets):
        for j in range(2):
            for way, sign in ways:
                wait1(j, 1 - way, 1, k)
                wait1(j, way, 2, k)
                mine = dkv_ref[j, place.slot(j == 0, 0, second), halves[way], :]
                mid[j, k, halves[way], :] = add(mine, box[j, 1 - way, 1, k], box[j, way, 2, k])
            if k == 0:
                for way, sign in ways:
                    send2(j, way, sign, 0, mid.at[j, 0, halves[way], :])
            if k in (1, 2):
                way, sign = ways[k - 1]
                send2(j, way, sign, 1, mid.at[j, k, halves[1 - way], :])
        if k == 1:
            ring.hop(0, 2)
    for j in range(2):
        for way, sign in ways:
            wait2(j, way, 0)
            box2[j, way, 0] = add(box2[j, way, 0], mid[j, 1 + way, halves[way], :])
            send2(j, way, sign, 2, box2.at[j, way, 0])
    ring.hop(0, 3)

    def gather(way, sign, j):
        recv = lambda kind: pool_recv.at[way, j, kind]
        return Gather(place, sender, 2 + j, pooled, recv, j, j != 0, way * half, half, sign, False)

    gathers = []
    for way, sign in ways:
        for j in range(2):
            wait2(j, 1 - way, 1)
            wait2(j, way, 2)
            pooled[j, place.seq, halves[way], :] = add(
                mid[j, 3, halves[way], :], box2[j, 1 - way, 1], box2[j, way, 2]
            )
            gathers.append(gather(way, sign, j))
            gathers[-1].begin()

    def near():
        for which in (1, 2):
            for one in gathers:
                one.near(which)

    def far():
        for one in gathers:
            one.far()

    def relay(i):
        for one in gathers:
            one.relay(i)

    def rest(i, second):
        for one in gathers:
            one.rest(i, second)

    def multiply(x, y):
        slot = place.slot(True, x, y)
        left = t[:, pl.ds(pl.multiple_of(slot * share, share), share), :].reshape(rows, feats)
        right = jnp.concatenate([pooled[0, slot], pooled[1, slot]], axis=1)
        product = dot_tn(left, right)
        dk_ref[...] += product[:, :cols]
        dv_ref[...] += product[:, cols:]

    near()
    ring.hop(0, 4)
    relay(0)
    arrived(t.at[pl.ds(0, RING)], send_sems.at[0], twin_recv.at[0], place.twin())
    multiply(0, 0)
    far()
    relay(1)
    relay(2)
    rest(0, 1)
    for step in (1, -1):
        multiply(step, 0)
        multiply(0, step)
    relay(3)
    rest(0, 2)
    multiply(2, 0)
    multiply(0, 2)
    rest(1, 1)
    rest(2, 1)
    for x in (1, -1):
        for y in (1, -1):
            multiply(x, y)
    rest(1, 2)
    rest(2, 2)
    rest(3, 1)
    for step in (1, -1):
        multiply(step, 2)
        multiply(2, step)
    rest(3, 2)
    multiply(2, 2)
    spare = (twin_recv.at[0], place.twin())
    sender.finish(box, 0, *spare)
    sender.finish(box2, 1, *spare)
    for j in range(2):
        sender.finish(pooled.at[j, pl.ds(0, 15)], 2 + j, *spare)
    sender.finish(t.at[pl.ds(0, RING - 1)], 4, *spare)
    sender.finish(t.at[pl.ds(0, RING)], 5, *spare)


def weight_grads(dkv, part):
    _, seqs, rows, cols = dkv.shape
    feats = part.shape[1]
    heads = 2 * RING
    half = rows // 2
    vmem = pl.BlockSpec(memory_space=pltpu.VMEM)
    dma = pltpu.SemaphoreType.DMA
    return pl.pallas_call(
        reduce_kernel,
        out_shape=(jax.ShapeDtypeStruct((feats, cols), jnp.float32),) * 2,
        in_specs=[vmem, vmem],
        out_specs=(vmem, vmem),
        scratch_shapes=[
            pltpu.VMEM((2, seqs, rows, cols), jnp.bfloat16),
            pltpu.VMEM((heads, rows, feats), jnp.bfloat16),
            pltpu.VMEM((2, 2, 3, SIDE, half, cols), jnp.bfloat16),
            pltpu.VMEM((2, SIDE, rows, cols), jnp.bfloat16),
            pltpu.VMEM((2, 2, 3, half, cols), jnp.bfloat16),
            dma((6,)),
            dma((2, 2, 3, SIDE)),
            dma((2, 2, 3)),
            dma((2, 2, 15)),
            dma((1,)),
            dma((2, RING // 2, 2)),
        ],
        compiler_params=pltpu.CompilerParams(
            collective_id=2, has_side_effects=True, vmem_limit_bytes=32 * MIB
        ),
        name="reduce_all",
    )(dkv, part)


def local(queries, states, key_weight, value_weight, neighbour_ids, out_grad):
    kv, part = pool(states, key_weight, value_weight)
    context, query_grad, dkv = attend(neighbour_ids.T, queries, out_grad, kv)
    dk, dv = weight_grads(dkv, part.reshape(states.shape))
    return context, query_grad, dk, dv


def solution(mesh):
    in_specs = (
        P("seq", "head"),
        P("seq", "head"),
        P(None, "head"),
        P(None, "head"),
        P("seq", None),
        P("seq", "head"),
    )
    out_specs = (P("seq", "head"), P("seq", "head"), P("seq", "head"), P("seq", "head"))
    return jax.shard_map(local, mesh=mesh, in_specs=in_specs, out_specs=out_specs, check_vma=False)
```

```python
import math

import jax
import jax.numpy as jnp
from jax import lax
from jax.experimental import pallas as pl
from jax.experimental.pallas import tpu as pltpu
from jax.sharding import PartitionSpec as P

HD = 128
SPAN = 64
NBR = 128
TOPN = 2
SCALE = 1.0 / math.sqrt(HD)
MIB = 1 << 20
MESH = pl.DeviceIdType.MESH
SIDE = 4
RING = 8
BATCHES = 4
ORDER = (
    ("start", 0), ("start", 1), ("hop", 0, 1, 0, 1), ("hop", 0, 1, 0, -1), ("hop", 0, 1, 1, 1), ("hop", 0, 1, 1, -1),
    ("twin", 0, -1), ("twin", 0, 1), ("hop", 1, 1, 0, 1), ("hop", 1, 1, 0, -1), ("hop", 1, 1, 1, 1),
    ("hop", 1, 1, 1, -1), ("twin", 1, -1), ("twin", 1, 1), ("other", 0, -1), ("other", 0, 0), ("own", 0, -1),
    ("hop", 0, 2, 0, 1), ("hop", 0, 2, 0, -1), ("own", 0, 0), ("own", 0, 1), ("other", 0, 1), ("hop", 0, 2, 1, 1),
    ("hop", 0, 2, 1, -1), ("twin", 0, -2), ("twin", 0, 2), ("own", 0, -2), ("own", 0, 2), ("other", 1, 0),
    ("hop", 1, 2, 0, 1), ("hop", 1, 2, 0, -1), ("own", 1, -1), ("own", 1, 0), ("own", 1, 1), ("hop", 1, 2, 1, 1),
    ("hop", 1, 2, 1, -1), ("twin", 1, -2), ("twin", 1, 2), ("other", 0, -2), ("other", 0, 2), ("hop", 0, 3, 0, 1),
    ("hop", 0, 3, 0, -1), ("own", 1, -2), ("own", 1, 2), ("other", 1, -1), ("hop", 0, 3, 1, 1), ("hop", 0, 3, 1, -1),
    ("twin", 0, -3), ("twin", 0, 3), ("own", 0, -3), ("own", 0, 3), ("other", 1, 1), ("hop", 1, 3, 0, 1),
    ("hop", 1, 3, 0, -1), ("other", 1, -2), ("other", 1, 2), ("own", 2, 0), ("hop", 1, 3, 1, 1), ("twin", 1, -3),
    ("hop", 1, 3, 1, -1), ("twin", 1, 3), ("other", 0, -3), ("start", 2), ("other", 0, 3), ("hop", 0, 4, 0, 1),
    ("own", 1, -3), ("own", 1, 3), ("own", 3, 0), ("hop", 0, 4, 1, -1), ("twin", 0, 4), ("own", 0, 4),
    ("other", 1, -3), ("start", 3), ("hop", 1, 4, 0, 1), ("other", 1, 3), ("other", 2, 0), ("hop", 1, 4, 1, -1),
    ("twin", 1, 4), ("other", 0, 4), ("project", 0), ("hop", 2, 1, 0, 1), ("hop", 2, 1, 0, -1), ("own", 1, 4),
    ("hop", 2, 1, 1, 1), ("twin", 2, -1), ("own", 2, -1), ("other", 3, 0), ("hop", 2, 1, 1, -1), ("twin", 2, 1),
    ("other", 1, 4), ("hop", 3, 1, 0, 1), ("project", 1), ("hop", 3, 1, 0, -1), ("hop", 3, 1, 1, 1), ("twin", 3, -1),
    ("own", 2, 1), ("other", 2, -1), ("hop", 3, 1, 1, -1), ("twin", 3, 1), ("near1", 0, 0), ("near2", 0, 0),
    ("relay", 0, 0, 0), ("hop", 2, 2, 0, 1), ("other", 2, 1), ("hop", 2, 2, 0, -1), ("relay", 0, 1, 0),
    ("near2", 0, 1), ("near1", 0, 1), ("hop", 2, 2, 1, 1), ("twin", 2, -2), ("hop", 2, 2, 1, -1), ("twin", 2, 2),
    ("own", 2, -2), ("own", 2, 2), ("near1", 1, 0), ("hop", 3, 2, 0, 1), ("near2", 1, 0), ("hop", 3, 2, 0, -1),
    ("relay", 1, 0, 0), ("own", 3, -1), ("own", 3, 1), ("hop", 3, 2, 1, 1), ("twin", 3, -2), ("relay", 1, 1, 0),
    ("hop", 3, 2, 1, -1), ("twin", 3, 2), ("near2", 1, 1), ("near1", 1, 1), ("far", 0, 0), ("hop", 2, 3, 0, 1),
    ("relay", 0, 0, 1), ("other", 2, -2), ("hop", 2, 3, 0, -1), ("other", 2, 2), ("own", 3, -2), ("hop", 2, 3, 1, 1),
    ("twin", 2, -3), ("relay", 0, 0, 2), ("hop", 2, 3, 1, -1), ("twin", 2, 3), ("relay", 0, 1, 2), ("own", 2, -3),
    ("own", 2, 3), ("hop", 3, 3, 0, 1), ("far", 0, 1), ("hop", 3, 3, 0, -1), ("relay", 0, 1, 1), ("own", 3, 2),
    ("other", 3, -1), ("hop", 3, 3, 1, 1), ("twin", 3, -3), ("relay", 1, 0, 1), ("other", 2, -3),
    ("hop", 3, 3, 1, -1), ("twin", 3, 3), ("far", 1, 0), ("relay", 1, 0, 2), ("hop", 2, 4, 0, 1), ("relay", 1, 1, 2),
    ("other", 2, 3), ("own", 3, -3), ("own", 3, 3), ("other", 3, 1), ("hop", 2, 4, 1, -1), ("twin", 2, 4),
    ("far", 1, 1), ("relay", 1, 1, 1), ("own", 2, 4), ("other", 3, -2), ("hop", 3, 4, 0, 1), ("relay", 0, 0, 3),
    ("other", 3, 2), ("other", 3, -3), ("other", 3, 3), ("other", 2, 4), ("hop", 3, 4, 1, -1), ("twin", 3, 4),
    ("project", 2), ("relay", 0, 1, 3), ("relay", 1, 0, 3), ("own", 3, 4), ("relay", 1, 1, 3), ("other", 3, 4),
    ("project", 3), ("swap", 0), ("near1", 2, 0), ("near2", 2, 0), ("relay", 2, 0, 0), ("relay", 2, 1, 0),
    ("near2", 2, 1), ("near1", 2, 1), ("near2", 3, 0), ("near1", 3, 0), ("relay", 3, 0, 0), ("near1", 3, 1),
    ("relay", 3, 1, 0), ("near2", 3, 1), ("swap", 1), ("relay", 2, 0, 1), ("far", 2, 0), ("relay", 2, 0, 2),
    ("relay", 2, 1, 2), ("relay", 2, 1, 1), ("far", 2, 1), ("relay", 3, 1, 1), ("far", 3, 0), ("relay", 3, 0, 2),
    ("relay", 3, 0, 1), ("far", 3, 1), ("relay", 3, 1, 2), ("relay", 2, 0, 3), ("relay", 3, 0, 3), ("relay", 2, 1, 3),
    ("relay", 3, 1, 3),
)


def dot_nt(a, b):
    return lax.dot_general(a, b, (((1,), (1,)), ((), ())), preferred_element_type=jnp.float32)


def dot_tn(a, b):
    return lax.dot_general(a, b, (((0,), (0,)), ((), ())), preferred_element_type=jnp.float32)


def dot_nn(a, b):
    return jnp.dot(a, b, preferred_element_type=jnp.float32)


def attend_kernel(ids_ref, q_ref, g_ref, kv_ref, ctx_out, dq_out, dkv_ref, acc_ref, ctx_ref, dq_ref, out_sems):
    cols = q_ref.shape[1]
    spans = q_ref.shape[0] // SPAN
    blocks = kv_ref.shape[1]
    first = lax.broadcasted_iota(jnp.int32, (SPAN, cols), 1) < HD

    def clear(i, _):
        for j in range(2):
            acc_ref[j, i] = jnp.zeros((NBR, cols), jnp.float32)
        return 0

    lax.fori_loop(0, blocks, clear, 0)

    def stack(x):
        zero = jnp.zeros_like(x)
        return jnp.concatenate([jnp.where(first, x, zero), jnp.where(first, zero, x)], axis=0)

    def unstack(x):
        return jnp.where(first, x[:SPAN], x[SPAN:])

    def span(c, _):
        rows = pl.ds(c * SPAN, SPAN)
        id0, id1 = ids_ref[0, c], ids_ref[1, c]
        keys = jnp.concatenate([kv_ref[0, id0], kv_ref[0, id1]], axis=0)
        values = jnp.concatenate([kv_ref[1, id0], kv_ref[1, id1]], axis=0)
        q2 = stack(q_ref[rows, :])
        g2 = stack(g_ref[rows, :])
        scores = dot_nt(q2, keys) * SCALE
        prob_grad = dot_nt(g2, values)
        top = jnp.max(scores, axis=-1, keepdims=True)
        e = jnp.exp(scores - top)
        probs = e * (1.0 / jnp.sum(e, axis=-1, keepdims=True))
        low = probs.astype(jnp.bfloat16)
        delta = jnp.sum(probs * prob_grad, axis=-1, keepdims=True)
        sg = (probs * (prob_grad - delta) * SCALE).astype(jnp.bfloat16)
        ctx_ref[rows, :] = unstack(dot_nn(low, values)).astype(jnp.bfloat16)
        dq_ref[rows, :] = unstack(dot_nn(sg, keys)).astype(jnp.bfloat16)
        dk = dot_tn(sg, q2)
        dv = dot_tn(low, g2)
        acc_ref[0, id0] += dk[:NBR]
        acc_ref[1, id0] += dv[:NBR]
        acc_ref[0, id1] += dk[NBR:]
        acc_ref[1, id1] += dv[NBR:]
        return 0

    lax.fori_loop(0, spans, span, 0, unroll=8)

    writes = [
        pltpu.make_async_copy(ctx_ref, ctx_out, out_sems.at[0]),
        pltpu.make_async_copy(dq_ref, dq_out, out_sems.at[1]),
    ]
    for write in writes:
        write.start()

    def store(i, _):
        for j in range(2):
            dkv_ref[j, i] = acc_ref[j, i].astype(jnp.bfloat16)
        return 0

    lax.fori_loop(0, blocks, store, 0)
    for write in writes:
        write.wait()


def attend(ids, queries, grads, kv):
    rows, cols = queries.shape
    blocks = kv.shape[1] * kv.shape[2] // NBR
    vmem, hbm = pl.BlockSpec(memory_space=pltpu.VMEM), pl.BlockSpec(memory_space=pltpu.HBM)
    context, query_grad, dkv = pl.pallas_call(
        attend_kernel,
        out_shape=(
            jax.ShapeDtypeStruct((rows, cols), jnp.bfloat16),
            jax.ShapeDtypeStruct((rows, cols), jnp.bfloat16),
            jax.ShapeDtypeStruct((2, blocks, NBR, cols), jnp.bfloat16),
        ),
        in_specs=[pl.BlockSpec(memory_space=pltpu.SMEM), vmem, vmem, vmem],
        out_specs=(hbm, hbm, vmem),
        scratch_shapes=[
            pltpu.VMEM((2, blocks, NBR, cols), jnp.float32),
            pltpu.VMEM((rows, cols), jnp.bfloat16),
            pltpu.VMEM((rows, cols), jnp.bfloat16),
            pltpu.SemaphoreType.DMA((2,)),
        ],
        compiler_params=pltpu.CompilerParams(vmem_limit_bytes=40 * MIB),
        name="attend",
    )(ids, queries, grads, kv.reshape(2, blocks, NBR, cols))
    return context, query_grad, dkv.reshape(kv.shape)


class Place:
    def __init__(self):
        self.seq = lax.axis_index("seq")
        self.head = lax.axis_index("head")
        x, z = lax.div(self.seq, SIDE), lax.div(self.head, 2)
        y, self.core = self.seq - x * SIDE, self.head - z * 2
        self.xs = [x] + [lax.rem(x + i, SIDE) for i in range(1, SIDE)]
        self.ys = [y] + [lax.rem(y + i, SIDE) for i in range(1, SIDE)]
        self.zs = [z] + [lax.rem(z + i, RING) for i in range(1, RING)]
        self.pairs = [2 * z for z in self.zs]
        self.rows = [SIDE * x for x in self.xs]
        self.other = (self.seq, self.pairs[0] + 1 - self.core)

    def along(self, is_x, step):
        return (self.slot(is_x, step, 0), self.head)

    def ring(self, step):
        return (self.seq, self.pairs[step % RING] + self.core)

    def twin(self):
        return self.other

    def slot(self, first_is_x, first, second):
        if not first_is_x:
            first, second = second, first
        return self.rows[first % SIDE] + self.ys[second % SIDE]


def greet(devices):
    barrier = pltpu.get_barrier_semaphore()
    for device in devices:
        pl.semaphore_signal(barrier, inc=1, device_id=device, device_id_type=MESH)
    pl.semaphore_wait(barrier, len(devices))


class Sender:
    def __init__(self, sems):
        self.sems = sems

    def send(self, src, dst, group, recv_sem, device):
        pltpu.make_async_remote_copy(
            src_ref=src,
            dst_ref=dst,
            send_sem=self.sems.at[group],
            recv_sem=recv_sem,
            device_id=device,
            device_id_type=MESH,
        ).start()

    def finish(self, ref, group, recv_sem, device):
        pltpu.make_async_remote_copy(
            src_ref=ref,
            dst_ref=ref,
            send_sem=self.sems.at[group],
            recv_sem=recv_sem,
            device_id=device,
            device_id_type=MESH,
        ).wait_send()


def arrived(ref, send_sem, recv_sem, device):
    pltpu.make_async_remote_copy(
        src_ref=ref, dst_ref=ref, send_sem=send_sem, recv_sem=recv_sem, device_id=device, device_id_type=MESH
    ).wait_recv()


class Gather:
    def __init__(self, place, sender, group, buf, recv, j, first_is_x, row, rows, sign, together):
        self.place, self.sender, self.group, self.buf, self.recv = place, sender, group, buf, recv
        self.j, self.fx, self.row, self.rows, self.sign, self.together = j, first_is_x, row, rows, sign, together

    def ref(self, slot):
        return self.buf.at[self.j, slot, pl.ds(self.row, self.rows), :]

    def send(self, offsets, kind, is_x, step):
        slot = self.place.slot(self.fx, *offsets)
        self.sender.send(self.ref(slot), self.ref(slot), self.group, self.recv(kind), self.place.along(is_x, step))

    def wait(self, offsets, kind):
        ref = self.ref(self.place.slot(self.fx, *offsets))
        arrived(ref, self.sender.sems.at[0], self.recv(kind), self.place.twin())

    def relays(self):
        return [0, -self.sign, self.sign, 2]

    def last(self, i, second):
        return 7 if self.together else 7 + 2 * i + second - 1

    def spread(self, i):
        first = self.relays()[i]
        self.send((first, 0), 3 + i, not self.fx, self.sign)
        self.send((first, 0), self.last(i, 1), not self.fx, -self.sign)

    def begin(self):
        self.send((0, 0), 0, self.fx, self.sign)
        self.send((0, 0), 1, self.fx, -self.sign)
        self.spread(0)

    def near(self, which):
        if which == 1:
            self.wait((-self.sign, 0), 0)
            self.send((-self.sign, 0), 2, self.fx, self.sign)
        else:
            self.wait((self.sign, 0), 1)
        self.spread(which)

    def far(self):
        self.wait((-2 * self.sign, 0), 2)
        self.spread(3)

    def relay(self, i):
        first = self.relays()[i]
        self.wait((first, -self.sign), 3 + i)
        self.send((first, -self.sign), self.last(i, 2), not self.fx, self.sign)

    def rest(self, i, second):
        self.wait((self.relays()[i], self.sign * second), self.last(i, second))


class Ring:
    def __init__(self, place, sender, groups, at, ring_recv, twin_recv, rows):
        self.place, self.sender, self.groups, self.at = place, sender, groups, at
        self.ring_recv, self.twin_recv, self.rows = ring_recv, twin_recv, rows

    def slot(self, distance, other):
        core = 1 - self.place.core if other else self.place.core
        return self.place.pairs[distance % RING] + core

    def unit(self, slot, b, u):
        half = self.rows // 2
        return self.at(slot, b * self.rows + u * half, half)

    def batch(self, slot, b):
        return self.at(slot, b * self.rows, self.rows)

    def signs(self, d, u):
        return (1, -1) if d < RING // 2 else ((1,) if u == 0 else (-1,))

    def ring_sem(self, sign, d, b, u):
        return self.ring_recv.at[0 if sign > 0 else 1, d - 1, 2 * b + u]

    def to_ring(self, slot, d, b, u, sign):
        ref = self.unit(slot, b, u)
        self.sender.send(ref, ref, self.groups[0] + b, self.ring_sem(sign, d, b, u), self.place.ring(sign))

    def to_twin(self, distance, b):
        ref = self.batch(self.slot(distance, False), b)
        self.sender.send(ref, ref, self.groups[1] + b, self.twin_recv(distance, b), self.place.twin())

    def start(self, b):
        for u in range(2):
            for sign in (1, -1):
                self.to_ring(self.place.head, 1, b, u, sign)
        self.to_twin(0, b)

    def relay(self, b, d, u, sign):
        slot = self.slot(-sign * d, False)
        arrived(self.unit(slot, b, u), self.sender.sems.at[0], self.ring_sem(sign, d, b, u), self.place.twin())
        if d < RING // 2 and sign in self.signs(d + 1, u):
            self.to_ring(slot, d + 1, b, u, sign)

    def hop(self, b, d):
        for u in range(2):
            for sign in self.signs(d, u):
                self.relay(b, d, u, sign)
        for distance in (-d, d) if d < RING // 2 else (d,):
            self.to_twin(distance, b)

    def from_twin(self, b, distance):
        slot = self.slot(distance, True)
        arrived(self.batch(slot, b), self.sender.sems.at[0], self.twin_recv(distance, b), self.place.twin())


def pool_kernel(
    states_ref, kw_ref, vw_ref, kv_ref, part_ref, st, shares, mid, w, acc,
    send_sems, twin_recv, ring_recv, pool_recv, swap_recv, w_sems,
):
    place = Place()
    rows, feats = st.shape[1:]
    cols = kv_ref.shape[3]
    batches = BATCHES
    batch = rows // batches
    loads = [pltpu.make_async_copy(kw_ref, w.at[0], w_sems.at[0]), pltpu.make_async_copy(vw_ref, w.at[1], w_sems.at[1])]
    own_states = pltpu.make_async_copy(states_ref, st.at[place.head], w_sems.at[2])
    own_states.start()
    for load in loads:
        load.start()
    acc[...] = jnp.zeros_like(acc)
    greet(
        [place.ring(1), place.ring(-1), place.twin()]
        + [place.along(i, d) for i in (True, False) for d in (1, -1, 2)]
    )
    sender = Sender(send_sems)

    def at(slot, row, n):
        return st.at[slot, pl.ds(row, n), :]

    def twin_sem(distance, b):
        return twin_recv.at[distance + RING // 2 - 1, b]

    ring = Ring(place, sender, (0, batches), at, ring_recv, twin_sem, batch)

    def multiply(slot, b):
        here = pl.ds(b * batch, batch)
        left = st[slot, here, :]
        acc[here, :cols] += dot_nn(left, w[0, slot])
        acc[here, cols:] += dot_nn(left, w[1, slot])

    def own(b, distance):
        multiply(ring.slot(distance, False), b)

    def other(b, distance):
        ring.from_twin(b, distance)
        multiply(ring.slot(distance, True), b)

    def twin(b, distance):
        ring.to_twin(distance, b)

    def project(b):
        here = pl.ds(b * batch, batch)
        kv_ref[0, place.seq, here, :] = acc[here, :cols].astype(kv_ref.dtype)
        kv_ref[1, place.seq, here, :] = acc[here, cols:].astype(kv_ref.dtype)
        for one in gathers[b]:
            one.begin()

    def gather(b, j):
        sign = 1 if (b + j) % 2 == 0 else -1
        recv = lambda kind: pool_recv.at[b, j, kind]
        return Gather(place, sender, 2 * batches + b, kv_ref, recv, j, j == 0, b * batch, batch, sign, True)

    gathers = [[gather(b, j) for j in range(2)] for b in range(batches)]

    share = rows // (SIDE * SIDE)
    mine = pl.ds(pl.multiple_of(place.head * share, share), share)
    side = [pl.ds(0, feats // 2), pl.ds(feats // 2, feats // 2)]
    here = (place.xs, place.ys)
    steps = (2, 1, -1)

    def gather_share():
        for slot in range(SIDE * SIDE):
            x, y = slot // SIDE, slot % SIDE
            shares[0, x, y] = st[slot, mine, side[0]]
            shares[1, y, x] = st[slot, mine, side[1]]

    def column(j, source):
        return part_ref.at[:, source, :, side[j]] if j == 0 else part_ref.at[source, :, :, side[j]]

    def swap_first():
        gather_share()
        for i, step in enumerate(steps):
            for j in range(2):
                sender.send(
                    shares.at[j, here[j][step % SIDE]], mid.at[j, here[j][0]], 3 * batches,
                    swap_recv.at[j, 0, i], place.along(j == 0, step),
                )
        for j in range(2):
            mid[j, here[j][0]] = shares[j, here[j][0]]

    def swap_second():
        for i, step in enumerate(steps):
            for j in range(2):
                arrived(mid.at[j, here[j][-step % SIDE]], send_sems.at[0], swap_recv.at[j, 0, i], place.twin())
        for i, step in enumerate(steps):
            for j in range(2):
                sender.send(
                    mid.at[j, :, here[1 - j][step % SIDE]], column(j, here[1 - j][0]), 3 * batches,
                    swap_recv.at[j, 1, i], place.along(j != 0, step),
                )
        for j in range(2):
            column(j, here[1 - j][0])[...] = mid[j, :, here[1 - j][0]]

    def swap_end():
        for i, step in enumerate(steps):
            for j in range(2):
                arrived(column(j, here[1 - j][-step % SIDE]), send_sems.at[0], swap_recv.at[j, 1, i], place.twin())

    steps_of = {
        "start": ring.start,
        "hop": ring.relay,
        "twin": twin,
        "own": own,
        "other": other,
        "project": project,
        "near1": lambda b, j: gathers[b][j].near(1),
        "near2": lambda b, j: gathers[b][j].near(2),
        "far": lambda b, j: gathers[b][j].far(),
        "relay": lambda b, j, i: gathers[b][j].relay(i),
        "swap": lambda i: (swap_first, swap_second)[i](),
    }
    own_states.wait()
    waiting = list(loads)
    for name, *what in ORDER:
        if name in ("own", "other") and waiting:
            for load in waiting:
                load.wait()
            waiting = []
        steps_of[name](*what)
    swap_end()
    for b in range(batches):
        for j in range(2):
            arrived(kv_ref.at[j, pl.ds(0, 8), pl.ds(0, batch), :], send_sems.at[0], pool_recv.at[b, j, 7], place.twin())
    spare = (swap_recv.at[0, 0, 0], place.twin())
    for b in range(batches):
        sender.finish(st.at[pl.ds(0, RING - 1), pl.ds(0, batch), :], b, *spare)
        sender.finish(st.at[pl.ds(0, RING), pl.ds(0, batch), :], batches + b, *spare)
        sender.finish(kv_ref.at[0, pl.ds(0, 15), pl.ds(0, 2 * batch), :], 2 * batches + b, *spare)
    sender.finish(st.at[pl.ds(0, 6), pl.ds(0, SIDE * share), :], 3 * batches, *spare)


def pool(states, key_weight, value_weight):
    rows, feats = states.shape
    cols = key_weight.shape[1]
    heads = key_weight.shape[0] // feats
    seqs = SIDE * SIDE
    share = rows // heads
    vmem, hbm = pl.BlockSpec(memory_space=pltpu.VMEM), pl.BlockSpec(memory_space=pltpu.HBM)
    dma = pltpu.SemaphoreType.DMA
    return pl.pallas_call(
        pool_kernel,
        out_shape=(
            jax.ShapeDtypeStruct((2, seqs, rows, cols), jnp.bfloat16),
            jax.ShapeDtypeStruct((SIDE, SIDE, share, feats), jnp.bfloat16),
        ),
        in_specs=[hbm, hbm, hbm],
        out_specs=(vmem, vmem),
        scratch_shapes=[
            pltpu.VMEM((heads, rows, feats), jnp.bfloat16),
            pltpu.VMEM((2, SIDE, SIDE, share, feats // 2), jnp.bfloat16),
            pltpu.VMEM((2, SIDE, SIDE, share, feats // 2), jnp.bfloat16),
            pltpu.VMEM((2, heads, feats, cols), jnp.bfloat16),
            pltpu.VMEM((rows, 2 * cols), jnp.float32),
            dma((3 * BATCHES + 1,)),
            dma((RING, BATCHES)),
            dma((2, RING // 2, 2 * BATCHES)),
            dma((BATCHES, 2, 8)),
            dma((2, 2, 3)),
            dma((3,)),
        ],
        compiler_params=pltpu.CompilerParams(
            collective_id=1, has_side_effects=True, vmem_limit_bytes=48 * MIB
        ),
        name="pool",
    )(states, key_weight.reshape(heads, feats, cols), value_weight.reshape(heads, feats, cols))


def reduce_kernel(
    dkv_ref, part_ref, dk_ref, dv_ref, pooled, t, box, mid, box2,
    send_sems, box_recv, box2_recv, pool_recv, twin_recv, ring_recv,
):
    place = Place()
    rows, cols = dkv_ref.shape[2], dkv_ref.shape[3]
    heads, feats = t.shape[0], t.shape[2]
    share = rows // heads
    half = rows // 2
    halves = (pl.ds(0, half), pl.ds(half, half))
    offsets = (2, 1, 3, 0)
    t[place.head] = part_ref[...]
    greet(
        [place.along(i, d) for i in (True, False) for d in (1, -1)] + [place.ring(1), place.ring(-1), place.twin()]
    )
    sender = Sender(send_sems)
    ways = ((0, 1), (1, -1))
    ring = Ring(
        place, sender, (4, 5), lambda slot, row, n: t.at[slot, pl.ds(row, n), :], ring_recv,
        lambda distance, b: twin_recv.at[0], rows,
    )

    def add(*terms):
        total = terms[0].astype(jnp.float32)
        for term in terms[1:]:
            total = total + term.astype(jnp.float32)
        return total.astype(jnp.bfloat16)

    def send1(j, way, sign, kind, k, src):
        sender.send(src, box.at[j, way, kind, k], 0, box_recv.at[j, way, kind, k], place.along(j == 0, sign))

    def wait1(j, way, kind, k):
        arrived(box.at[j, way, kind, k], send_sems.at[0], box_recv.at[j, way, kind, k], place.along(j == 0, 1))

    def send2(j, way, sign, kind, src):
        sender.send(src, box2.at[j, way, kind], 1, box2_recv.at[j, way, kind], place.along(j != 0, sign))

    def wait2(j, way, kind):
        arrived(box2.at[j, way, kind], send_sems.at[0], box2_recv.at[j, way, kind], place.along(j != 0, 1))

    for k, second in enumerate(offsets):
        for j in range(2):
            for way, sign in ways:
                send1(j, way, sign, 0, k, dkv_ref.at[j, place.slot(j == 0, 2, second), halves[way], :])
    for k, second in enumerate(offsets):
        for j in range(2):
            for way, sign in ways:
                send1(j, way, sign, 1, k, dkv_ref.at[j, place.slot(j == 0, sign, second), halves[1 - way], :])
    ring.start(0)
    for k, second in enumerate(offsets):
        for j in range(2):
            for way, sign in ways:
                wait1(j, way, 0, k)
                mine = dkv_ref[j, place.slot(j == 0, sign, second), halves[way], :]
                box[j, way, 0, k] = add(box[j, way, 0, k], mine)
                send1(j, way, sign, 2, k, box.at[j, way, 0, k])
    dk_ref[...] = jnp.zeros_like(dk_ref)
    dv_ref[...] = jnp.zeros_like(dv_ref)
    ring.hop(0, 1)
    for k, second in enumerate(offsets):
        for j in range(2):
            for way, sign in ways:
                wait1(j, 1 - way, 1, k)
                wait1(j, way, 2, k)
                mine = dkv_ref[j, place.slot(j == 0, 0, second), halves[way], :]
                mid[j, k, halves[way], :] = add(mine, box[j, 1 - way, 1, k], box[j, way, 2, k])
            if k == 0:
                for way, sign in ways:
                    send2(j, way, sign, 0, mid.at[j, 0, halves[way], :])
            if k in (1, 2):
                way, sign = ways[k - 1]
                send2(j, way, sign, 1, mid.at[j, k, halves[1 - way], :])
        if k == 1:
            ring.hop(0, 2)
    for j in range(2):
        for way, sign in ways:
            wait2(j, way, 0)
            box2[j, way, 0] = add(box2[j, way, 0], mid[j, 1 + way, halves[way], :])
            send2(j, way, sign, 2, box2.at[j, way, 0])
    ring.hop(0, 3)

    def gather(way, sign, j):
        recv = lambda kind: pool_recv.at[way, j, kind]
        return Gather(place, sender, 2 + j, pooled, recv, j, j != 0, way * half, half, sign, False)

    gathers = []
    for way, sign in ways:
        for j in range(2):
            wait2(j, 1 - way, 1)
            wait2(j, way, 2)
            pooled[j, place.seq, halves[way], :] = add(
                mid[j, 3, halves[way], :], box2[j, 1 - way, 1], box2[j, way, 2]
            )
            gathers.append(gather(way, sign, j))
            gathers[-1].begin()

    def near():
        for which in (1, 2):
            for one in gathers:
                one.near(which)

    def far():
        for one in gathers:
            one.far()

    def relay(i):
        for one in gathers:
            one.relay(i)

    def rest(i, second):
        for one in gathers:
            one.rest(i, second)

    def multiply(x, y):
        slot = place.slot(True, x, y)
        left = t[:, pl.ds(pl.multiple_of(slot * share, share), share), :].reshape(rows, feats)
        right = jnp.concatenate([pooled[0, slot], pooled[1, slot]], axis=1)
        product = dot_tn(left, right)
        dk_ref[...] += product[:, :cols]
        dv_ref[...] += product[:, cols:]

    near()
    ring.hop(0, 4)
    relay(0)
    arrived(t.at[pl.ds(0, RING)], send_sems.at[0], twin_recv.at[0], place.twin())
    multiply(0, 0)
    far()
    relay(1)
    relay(2)
    rest(0, 1)
    for step in (1, -1):
        multiply(step, 0)
        multiply(0, step)
    relay(3)
    rest(0, 2)
    multiply(2, 0)
    multiply(0, 2)
    rest(1, 1)
    rest(2, 1)
    for x in (1, -1):
        for y in (1, -1):
            multiply(x, y)
    rest(1, 2)
    rest(2, 2)
    rest(3, 1)
    for step in (1, -1):
        multiply(step, 2)
        multiply(2, step)
    rest(3, 2)
    multiply(2, 2)
    spare = (twin_recv.at[0], place.twin())
    sender.finish(box, 0, *spare)
    sender.finish(box2, 1, *spare)
    for j in range(2):
        sender.finish(pooled.at[j, pl.ds(0, 15)], 2 + j, *spare)
    sender.finish(t.at[pl.ds(0, RING - 1)], 4, *spare)
    sender.finish(t.at[pl.ds(0, RING)], 5, *spare)


def weight_grads(dkv, part):
    _, seqs, rows, cols = dkv.shape
    feats = part.shape[1]
    heads = 2 * RING
    half = rows // 2
    vmem = pl.BlockSpec(memory_space=pltpu.VMEM)
    dma = pltpu.SemaphoreType.DMA
    return pl.pallas_call(
        reduce_kernel,
        out_shape=(jax.ShapeDtypeStruct((feats, cols), jnp.float32),) * 2,
        in_specs=[vmem, vmem],
        out_specs=(vmem, vmem),
        scratch_shapes=[
            pltpu.VMEM((2, seqs, rows, cols), jnp.bfloat16),
            pltpu.VMEM((heads, rows, feats), jnp.bfloat16),
            pltpu.VMEM((2, 2, 3, SIDE, half, cols), jnp.bfloat16),
            pltpu.VMEM((2, SIDE, rows, cols), jnp.bfloat16),
            pltpu.VMEM((2, 2, 3, half, cols), jnp.bfloat16),
            dma((6,)),
            dma((2, 2, 3, SIDE)),
            dma((2, 2, 3)),
            dma((2, 2, 15)),
            dma((1,)),
            dma((2, RING // 2, 2)),
        ],
        compiler_params=pltpu.CompilerParams(
            collective_id=2, has_side_effects=True, vmem_limit_bytes=32 * MIB
        ),
        name="reduce_all",
    )(dkv, part)


def local(queries, states, key_weight, value_weight, neighbour_ids, out_grad):
    kv, part = pool(states, key_weight, value_weight)
    context, query_grad, dkv = attend(neighbour_ids.T, queries, out_grad, kv)
    dk, dv = weight_grads(dkv, part.reshape(states.shape))
    return context, query_grad, dk, dv


def solution(mesh):
    in_specs = (
        P("seq", "head"),
        P("seq", "head"),
        P(None, "head"),
        P(None, "head"),
        P("seq", None),
        P("seq", "head"),
    )
    out_specs = (P("seq", "head"), P("seq", "head"), P("seq", "head"), P("seq", "head"))
    return jax.shard_map(local, mesh=mesh, in_specs=in_specs, out_specs=out_specs, check_vma=False)
```
